128 devices in a mesh: lat: 8 (over x_lo, z), lon: 16 (over x_hi, y, core).
Axes of the slice: x: 4 (x_hi: 2, x_lo: 2; x = x_hi * 2 + x_lo), y: 4, z: 4, core: 2. Of those that a mesh axis runs over, the one named last changes fastest.
Arguments:
- wind_u: float32 [8, 512, 12000], P(None, 'lat', 'lon'), may hold values from -6 to 6
- wind_v: float32 [8, 512, 12000], P(None, 'lat', 'lon'), may hold values from -6 to 6
- tracer: float32 [8, 512, 12000], P(None, 'lat', 'lon'), may hold values from -6 to 6
- cutoff: int32 [512], P('lat'), may hold values from 1 to 1024, as said below
- row_scale: float32 [512], P('lat'), may hold values from 1 to 10
Outputs:
- tracer_next: float32 [8, 512, 12000], P(None, 'lat', 'lon')
- divergence: float32 [8, 512, 12000], P(None, 'lat', 'lon')
- vorticity: float32 [8, 512, 12000], P(None, 'lat', 'lon')
The draws below stay inside these ranges and needn't reach their ends.
Inputs may be any that keep to these rules, and one draw needn't show every extreme that they name: cutoff of row r is min(1024, 1024 * (r + 1) // 512 + j) with a whole j from 0 to 63 drawn per row, and at least 1; the last row's is 1024.
All inputs are finite; a program needn't handle non-finite values.
Results may differ from the reference program's by a relative error of at most 0.00014.
Values sent between devices are 32-bit elements; how exact they have to be, the bound alone decides.
A program may use at most 128 MiB of HBM per device.

```python
import math
import jax
import jax.numpy as jnp

NLON = 12000
LEV = 8
KMAX = 1024
NSLAB = 512


def draw_cutoff(key, part):
    rows = jnp.arange(NSLAB, dtype=jnp.int32)
    base = KMAX * (rows + 1) // NSLAB
    jitter = jax.random.randint(jax.random.fold_in(key, 7), (NSLAB,), 0, 64)
    return jnp.clip(base + jitter, 1, KMAX).astype(jnp.int32)


def block_scale(own_key, shape, pieces, least, top_value):
    def one(axis_at, blocks):
        heights = jax.random.uniform(jax.random.fold_in(jax.random.fold_in(own_key, 6), axis_at), (blocks,), jnp.float32, least / len(pieces), top_value / len(pieces))
        return jnp.repeat(jnp.exp(heights), shape[axis_at] // blocks).reshape((-1,) + (1,) * (len(shape) - axis_at - 1))

    gain = one(*pieces[0])
    for cut in pieces[1:]:
        gain = gain * one(*cut)
    return gain


def scatter_about(stream_key, extent, spread, bound, shards=(), held_as=jnp.bfloat16):
    level = block_scale(stream_key, extent, shards, -0.22, 0.18) if shards else 1.0
    drawn = jax.random.normal(stream_key, extent, jnp.float32) * spread * level
    return jnp.minimum(jnp.maximum(drawn, -bound), bound).astype(held_as)


def setup_inputs(seed: int = 0) -> dict:
    streams_of = jax.random.split(jax.random.key(seed), 6)
    return {
        "wind_u": scatter_about(streams_of[0], (LEV, NSLAB, NLON), 1.0, 6.0, ((1, 8), (2, 16)), jnp.float32),
        "wind_v": scatter_about(streams_of[1], (LEV, NSLAB, NLON), 1.0, 6.0, ((1, 8), (2, 16)), jnp.float32),
        "tracer": scatter_about(streams_of[2], (LEV, NSLAB, NLON), 1.0, 6.0, ((1, 8), (2, 16)), jnp.float32),
        "cutoff": draw_cutoff(jax.random.fold_in(streams_of[5], 71), 0),
        "row_scale": jnp.clip(jnp.exp(math.log(10.0) - 2.3025851 * jax.random.uniform(streams_of[4], (NSLAB,), jnp.float32) ** block_scale(streams_of[4], (NSLAB,), ((0, 8),), -0.2, 0.2)), 1.0, 10.0),
    }


courant = 0.5


def filter_field(field, keep):
    spectrum = jnp.fft.rfft(field, axis=-1)[..., :KMAX] * keep[None]
    return jnp.fft.irfft(spectrum, n=NLON, axis=-1).astype(jnp.float32)


def east_west(field):
    return jnp.roll(field, -1, axis=2) - jnp.roll(field, 1, axis=2)


def north_south(field):
    padded = jnp.pad(field, ((0, 0), (1, 1), (0, 0)))
    return padded[:, 2:] - padded[:, :-2]


def reference(wind_u, wind_v, tracer, cutoff, row_scale):
    numbers = jnp.arange(KMAX, dtype=jnp.int32)
    keep = (numbers[None, :] < cutoff[:, None]).astype(jnp.float32)
    filt_u = filter_field(wind_u, keep)
    filt_v = filter_field(wind_v, keep)
    filt_q = filter_field(tracer, keep)
    metric = row_scale[None, :, None]
    divergence = metric * (east_west(filt_u) + north_south(filt_v / metric))
    vorticity = metric * (east_west(filt_v) - north_south(filt_u / metric))
    tracer_next = tracer - courant * (filt_u * metric * east_west(filt_q) + filt_v * north_south(filt_q))
    return tracer_next, divergence, vorticity
```

```python
import functools
import math

import numpy as np
import jax
import jax.numpy as jnp
from jax import lax
from jax.experimental import pallas as pl
from jax.experimental.pallas import tpu as pltpu
from jax.sharding import PartitionSpec as P

NLON = 12000
SEG = 750
PAD = 768
LANES = 128
MESH = pl.DeviceIdType.MESH
F32 = jnp.float32
BF16 = jnp.bfloat16
ROOT_HALF = math.sqrt(0.5)
courant = 0.5


def phase(steps):
    angle = 2.0 * np.pi * (np.asarray(steps, dtype=np.int64) % NLON) / NLON
    return np.stack([np.cos(angle), np.sin(angle)]).astype(np.float32)


def small_tables():
    k2 = np.arange(128)
    start = (750 * np.arange(2)[:, None] + 32 * np.arange(24)[None, :]).reshape(48)
    inner = np.arange(32)
    last = np.where(inner == 31, -1 - 736, inner)
    coarse, fine = [], []
    for mult in (8 * k2, 8 * k2 + 4):
        coarse.append(phase(start[:, None] * mult[None, :]))
        fine.append(np.stack([phase(b[:, None] * mult[None, :]) for b in (inner, last)]))
    lanes = np.arange(PAD)
    lanes = np.where(lanes == PAD - 1, -1, lanes)
    place = 750 * np.arange(2)[:, None] + lanes[None, :]
    twiddle = np.stack([phase(k1 * place) for k1 in (1, 2, 3)])
    return np.stack(coarse), np.stack(fine), twiddle[:, :, :, None, :]


def split(values):
    high = values.astype(BF16)
    return high, (values - high.astype(F32)).astype(BF16)


def dot3(high, low, table_high, table_low, dims):
    def one(a, b):
        return lax.dot_general(a, b, (dims, ((), ())), preferred_element_type=F32)

    return one(high, table_high) + (one(high, table_low) + one(low, table_high))


def filter_kernel(
    u_ref, v_ref, q_ref, cut_ref, scale_ref, coarse_ref, fine_ref, tw_ref,
    filt_ref, edge_ref,
    raw, table_h, table_l, y_h, y_l, prod, zed, back, edge_out,
    fs, fr, bs, br, es, er, loc,
):
    lat = lax.axis_index("lat")
    me = lax.axis_index("lon")
    row_group, level_half = me % 8, me // 8
    fields = (u_ref, v_ref, q_ref)

    def block_of(ref, member):
        return ref.at[pl.ds(4 * (member // 8), 4), pl.ds(pl.multiple_of(8 * (member % 8), 8), 8)]

    def forward(f, i):
        dest = (me + i) % 16
        return pltpu.make_async_remote_copy(
            src_ref=block_of(fields[f], dest), dst_ref=raw.at[f, me],
            send_sem=fs.at[f, i], recv_sem=fr.at[f, i],
            device_id={"lon": dest}, device_id_type=MESH,
        )

    def own_forward(f):
        return pltpu.make_async_copy(block_of(fields[f], me), raw.at[f, me], loc.at[f])

    def backward(f, i):
        dest = (me + i) % 16
        return pltpu.make_async_remote_copy(
            src_ref=back.at[f, dest], dst_ref=block_of(filt_ref.at[f], me),
            send_sem=bs.at[f, i], recv_sem=br.at[f, i],
            device_id={"lon": dest}, device_id_type=MESH,
        )

    def own_backward(f):
        return pltpu.make_async_copy(back.at[f, me], block_of(filt_ref.at[f], me), loc.at[3 + f])

    def edge(f, side, i):
        dest = (me + i) % 16
        return pltpu.make_async_remote_copy(
            src_ref=edge_out.at[f, dest], dst_ref=edge_ref.at[f, side, pl.ds(4 * level_half, 4)],
            send_sem=es.at[f, i], recv_sem=er.at[f, side, level_half],
            device_id={"lat": lat + (1 - 2 * side), "lon": dest}, device_id_type=MESH,
        )

    sends_down = jnp.logical_and(row_group == 7, lat < 7)
    sends_up = jnp.logical_and(row_group == 0, lat > 0)

    for f in range(3):
        own_forward(f).start()

        def start(i, carry, f=f):
            forward(f, i).start()
            return carry

        lax.fori_loop(1, 16, start, 0)

    for kind in range(2):
        for c in range(2):
            def fill(a, carry, kind=kind, c=c):
                tail = jnp.where(a == 23, 1, 0)
                c1 = coarse_ref[kind, 0, pl.ds(24 * c + a, 1), :]
                s1 = coarse_ref[kind, 1, pl.ds(24 * c + a, 1), :]
                c2 = fine_ref[kind, tail, 0]
                s2 = fine_ref[kind, tail, 1]
                rows = pl.ds(pl.multiple_of(32 * a, 32), 32)
                for side, value in enumerate((c1 * c2 - s1 * s2, s1 * c2 + c1 * s2)):
                    high, low = split(value)
                    cols = pl.ds(128 * side, 128)
                    table_h[kind, c, rows, cols] = high
                    table_l[kind, c, rows, cols] = low
                return carry

            lax.fori_loop(0, 24, fill, 0)
    y_h[...] = jnp.zeros_like(y_h)
    y_l[...] = jnp.zeros_like(y_l)

    row_at = lax.broadcasted_iota(jnp.int32, (8, 256), 0)
    limits = jnp.zeros((8, 256), jnp.int32)
    for row in range(8):
        limits = jnp.where(row_at == row, cut_ref[8 * row_group + row], limits)
    k2 = lax.broadcasted_iota(jnp.int32, (8, 256), 1) % 128
    sign = jnp.where(lax.broadcasted_iota(jnp.int32, (8, 256), 1) < 128, 1.0, -1.0).astype(F32)
    weight = 2.0 / NLON

    def kept(k):
        return jnp.where(k < limits, F32(weight), F32(0.0))

    for f in range(3):
        own_forward(f).wait()

        def arrive(i, carry, f=f):
            forward(f, i).wait_recv()
            return carry

        lax.fori_loop(1, 16, arrive, 0)

        def analyse(pair, carry, f=f):
            lines = pl.ds(pl.multiple_of(16 * pair, 16), 16)
            for c in range(2):
                for lo in range(0, SEG, LANES):
                    hi = min(SEG, lo + LANES)
                    x = [
                        raw[f, 2 * d + c, pl.ds(2 * pair, 2), :, lo:hi].reshape(16, hi - lo)
                        for d in range(8)
                    ]
                    s = [x[d] + x[d + 4] for d in range(4)]
                    t = [x[d] - x[d + 4] for d in range(4)]
                    s02, s13 = s[0] + s[2], s[1] + s[3]
                    minus, plus = (t[3] - t[1]) * ROOT_HALF, (t[1] + t[3]) * -ROOT_HALF
                    parts = (
                        (t[0] + minus, -t[2] - plus),
                        (s[0] - s[2], s[1] - s[3]),
                        (t[0] - minus, t[2] - plus),
                    )
                    rows = [s02 - s13]
                    for k1 in range(3):
                        re, im = parts[k1]
                        co = tw_ref[k1, 0, c, :, lo:hi]
                        si = tw_ref[k1, 1, c, :, lo:hi]
                        rows += [re * co + im * si, im * co - re * si]
                    rows.append(s02 + s13)
                    for r, value in enumerate(rows):
                        high, low = split(value)
                        y_h[c, r, lines, lo:hi] = high
                        y_l[c, r, lines, lo:hi] = low
            return carry

        lax.fori_loop(0, 2, analyse, 0)

        for kind, r0, r1 in ((1, 0, 7), (0, 7, 8)):
            total = None
            for c in range(2):
                part = dot3(
                    y_h[c, r0:r1].reshape((r1 - r0) * 32, PAD), y_l[c, r0:r1].reshape((r1 - r0) * 32, PAD),
                    table_h[kind, c], table_l[kind, c], ((1,), (0,)),
                )
                total = part if total is None else total + part
            prod[r0:r1] = total.reshape(r1 - r0, 32, 256)

        def keep(level, carry):
            lines = pl.ds(pl.multiple_of(8 * level, 8), 8)
            zero = jnp.where(k2 == 0, F32(0.5), F32(1.0))
            prod[0, lines, :] = prod[0, lines, :] * kept(8 * k2 + 4)
            prod[7, lines, :] = prod[7, lines, :] * (kept(8 * k2) * zero)
            for k1 in (1, 2, 3):
                above, below = kept(8 * k2 + 4 + k1), kept(8 * k2 + 4 - k1)
                both, odd = above + below, (above - below) * sign
                r1, r2 = prod[2 * k1 - 1, lines, :], prod[2 * k1, lines, :]
                swap1 = jnp.concatenate([r1[:, 128:], r1[:, :128]], axis=1)
                swap2 = jnp.concatenate([r2[:, 128:], r2[:, :128]], axis=1)
                prod[2 * k1 - 1, lines, :] = both * r1 + odd * swap2
                prod[2 * k1, lines, :] = both * r2 - odd * swap1
            return carry

        lax.fori_loop(0, 4, keep, 0)

        for kind, r0, r1 in ((1, 0, 7), (0, 7, 8)):
            high, low = split(prod[r0:r1].reshape((r1 - r0) * 32, 256))
            for c in range(2):
                zed[c, r0:r1] = dot3(
                    high, low, table_h[kind, c], table_l[kind, c], ((1,), (1,))
                ).reshape(r1 - r0, 32, PAD)

        def synthesise(level, carry, f=f):
            lines = pl.ds(pl.multiple_of(8 * level, 8), 8)
            for c in range(2):
                for lo in range(0, PAD, LANES):
                    hi = lo + LANES
                    z = [zed[c, r, lines, lo:hi] for r in range(8)]
                    v = []
                    for k1 in range(3):
                        co = tw_ref[k1, 0, c, :, lo:hi]
                        si = tw_ref[k1, 1, c, :, lo:hi]
                        re, im = z[2 * k1 + 1], z[2 * k1 + 2]
                        v.append((re * co - im * si, im * co + re * si))
                    (ar, ai), (br_, bi), (cr, ci) = v
                    up, down = z[0] + z[7], z[0] - z[7]
                    even = (up + br_, down - bi, up - br_, down + bi)
                    p, m = (ar - cr) * ROOT_HALF, (ai + ci) * ROOT_HALF
                    odd = (ar + cr, p - m, ci - ai, -p - m)
                    for d in range(4):
                        one, other = even[d] + odd[d], even[d] - odd[d]
                        back[f, 2 * d + c, level, :, lo:hi] = one if d % 2 == 0 else -one
                        back[f, 2 * d + 8 + c, level, :, lo:hi] = other if d % 2 == 0 else -other
            return carry

        lax.fori_loop(0, 4, synthesise, 0)

        own_backward(f).start()

        def send(i, carry, f=f):
            backward(f, i).start()
            return carry

        lax.fori_loop(1, 16, send, 0)

        for side, sends, row in ((0, sends_down, 7), (1, sends_up, 0)):
            @pl.when(sends)
            def _(f=f, side=side, row=row):
                factor = 1.0 / jnp.full((1, PAD), scale_ref[8 * row_group + row], F32) if f < 2 else None

                def pack(member, carry):
                    for level in range(4):
                        value = back[f, member, level, row:row + 1, :]
                        edge_out[f, member, level] = value if factor is None else value * factor
                    return carry

                lax.fori_loop(0, 16, pack, 0)

                def post(i, carry):
                    edge(f, side, i).start()
                    return carry

                lax.fori_loop(0, 16, post, 0)

    for f in range(3):
        own_backward(f).wait()

        def finish(i, carry, f=f):
            forward(f, i).wait_send()
            backward(f, i).wait_send()
            backward(f, i).wait_recv()
            return carry

        lax.fori_loop(1, 16, finish, 0)
        for side, sends, gets in ((0, sends_down, lat > 0), (1, sends_up, lat < 7)):
            @pl.when(sends)
            def _(f=f, side=side):
                def sent(i, carry):
                    edge(f, side, i).wait_send()
                    return carry

                lax.fori_loop(0, 16, sent, 0)

            @pl.when(gets)
            def _(f=f, side=side):
                for half in range(2):
                    pltpu.make_async_remote_copy(
                        src_ref=edge_out.at[f, 0], dst_ref=edge_ref.at[f, side, pl.ds(4 * half, 4)],
                        send_sem=es.at[f, 0], recv_sem=er.at[f, side, half],
                        device_id={"lat": lat, "lon": (me + 1) % 16}, device_id_type=MESH,
                    ).wait_recv()


def stencil_kernel(filt_ref, edge_ref, tracer_ref, row_scale_ref, t_ref, d_ref, z_ref, scale_ref, inv_ref):
    lat = lax.axis_index("lat")

    @pl.when(pl.program_id(0) == 0)
    def _():
        def spread(row, carry):
            scale_ref[pl.ds(row, 1), :] = jnp.full((1, LANES), row_scale_ref[row], F32)
            return carry

        lax.fori_loop(0, 64, spread, 0, unroll=8)
        inv_ref[...] = 1.0 / scale_ref[...]

    scale = jnp.concatenate([scale_ref[...]] * (PAD // LANES), axis=1)
    inv = jnp.concatenate([inv_ref[...]] * (PAD // LANES), axis=1)
    first = lax.broadcasted_iota(jnp.int32, (64, PAD), 0) == 0
    last = lax.broadcasted_iota(jnp.int32, (64, PAD), 0) == 63

    def change(field, values):
        above = jnp.where(lat > 0, edge_ref[field, 0, 0], F32(0.0))
        below = jnp.where(lat < 7, edge_ref[field, 1, 0], F32(0.0))
        north = jnp.where(first, above, pltpu.roll(values, 1, 0))
        south = jnp.where(last, below, pltpu.roll(values, 63, 0))
        return south - north

    def east_west(values):
        return pltpu.roll(values, PAD - 1, 1) - pltpu.roll(values, 1, 1)

    u, v, q = filt_ref[0, 0], filt_ref[1, 0], filt_ref[2, 0]
    d_ref[0] = (scale * (east_west(u) + change(1, v * inv)))[:, :SEG]
    z_ref[0] = (scale * (east_west(v) - change(0, u * inv)))[:, :SEG]
    flux = u * scale * east_west(q) + v * change(2, q)
    t_ref[0] = tracer_ref[0] - courant * flux[:, :SEG]


def on_device(tables, wind_u, wind_v, tracer, cutoff, row_scale):
    coarse, fine, twiddle = (jnp.asarray(t) for t in tables)
    hbm = pl.BlockSpec(memory_space=pl.ANY)
    vmem = pl.BlockSpec(memory_space=pltpu.VMEM)
    smem = pl.BlockSpec(memory_space=pltpu.SMEM)
    dma = pltpu.SemaphoreType.DMA
    filt, edge = pl.pallas_call(
        filter_kernel,
        name="polar_filter",
        out_shape=(
            jax.ShapeDtypeStruct((3, 8, 64, PAD), F32),
            jax.ShapeDtypeStruct((3, 2, 8, 1, PAD), F32),
        ),
        in_specs=[hbm, hbm, hbm, smem, smem, vmem, vmem, vmem],
        out_specs=(hbm, hbm),
        scratch_shapes=[
            pltpu.VMEM((3, 16, 4, 8, SEG), F32),
            pltpu.VMEM((2, 2, PAD, 256), BF16),
            pltpu.VMEM((2, 2, PAD, 256), BF16),
            pltpu.VMEM((2, 8, 32, PAD), BF16),
            pltpu.VMEM((2, 8, 32, PAD), BF16),
            pltpu.VMEM((8, 32, 256), F32),
            pltpu.VMEM((2, 8, 32, PAD), F32),
            pltpu.VMEM((3, 16, 4, 8, PAD), F32),
            pltpu.VMEM((3, 16, 4, 1, PAD), F32),
            dma((3, 16)), dma((3, 16)), dma((3, 16)), dma((3, 16)),
            dma((3, 16)), dma((3, 2, 2)), dma((6,)),
        ],
        compiler_params=pltpu.CompilerParams(has_side_effects=True, vmem_limit_bytes=60 * 1024 * 1024),
    )(wind_u, wind_v, tracer, cutoff, row_scale, coarse, fine, twiddle)
    level = pl.BlockSpec((1, 64, SEG), lambda k: (k, 0, 0))
    shape = jax.ShapeDtypeStruct((8, 64, SEG), F32)
    return pl.pallas_call(
        stencil_kernel,
        name="flux_stencil",
        grid=(8,),
        out_shape=(shape, shape, shape),
        in_specs=[
            pl.BlockSpec((3, 1, 64, PAD), lambda k: (0, k, 0, 0)),
            pl.BlockSpec((3, 2, 1, 1, PAD), lambda k: (0, 0, k, 0, 0)),
            level, smem,
        ],
        out_specs=(level, level, level),
        scratch_shapes=[pltpu.VMEM((64, LANES), F32), pltpu.VMEM((64, LANES), F32)],
    )(filt, edge, tracer, row_scale)


def solution(mesh):
    in_specs = (
        P(None, "lat", "lon"),
        P(None, "lat", "lon"),
        P(None, "lat", "lon"),
        P("lat"),
        P("lat"),
    )
    out_specs = (P(None, "lat", "lon"), P(None, "lat", "lon"), P(None, "lat", "lon"))
    return jax.shard_map(
        functools.partial(on_device, small_tables()),
        mesh=mesh, in_specs=in_specs, out_specs=out_specs, check_vma=False,
    )
```

```python
import functools
import math

import numpy as np
import jax
import jax.numpy as jnp
from jax import lax
from jax.experimental import pallas as pl
from jax.experimental.pallas import tpu as pltpu
from jax.sharding import PartitionSpec as P

NLON = 12000
SEG = 750
PAD = 768
LANES = 128
MESH = pl.DeviceIdType.MESH
F32 = jnp.float32
BF16 = jnp.bfloat16
ROOT_HALF = math.sqrt(0.5)
courant = 0.5


def phase(steps):
    angle = 2.0 * np.pi * (np.asarray(steps, dtype=np.int64) % NLON) / NLON
    return np.stack([np.cos(angle), np.sin(angle)]).astype(np.float32)


def small_tables():
    k2 = np.arange(128)
    start = (750 * np.arange(2)[:, None] + 32 * np.arange(24)[None, :]).reshape(48)
    inner = np.arange(32)
    last = np.where(inner == 31, -1 - 736, inner)
    coarse, fine = [], []
    for mult in (8 * k2, 8 * k2 + 4):
        coarse.append(phase(start[:, None] * mult[None, :]))
        fine.append(np.stack([phase(b[:, None] * mult[None, :]) for b in (inner, last)]))
    lanes = np.arange(PAD)
    lanes = np.where(lanes == PAD - 1, -1, lanes)
    place = 750 * np.arange(2)[:, None] + lanes[None, :]
    twiddle = np.stack([np.stack([phase(k1 * (1500 * d + place)) for k1 in (1, 2, 3)]) for d in range(8)])
    return np.stack(coarse), np.stack(fine), twiddle[:, :, :, :, None, :]


def split(values):
    high = values.astype(BF16)
    return high, (values - high.astype(F32)).astype(BF16)


def dot3(high, low, table_high, table_low, dims):
    def one(a, b):
        return lax.dot_general(a, b, (dims, ((), ())), preferred_element_type=F32)

    return one(high, table_high) + (one(high, table_low) + one(low, table_high))


def filter_kernel(
    u_ref, v_ref, q_ref, cut_ref, scale_ref, coarse_ref, fine_ref, tw_ref,
    filt_ref, edge_ref,
    raw_u, raw_x, table, y_h, y_l, zed,
    prod_u, peer_u, spec_u, prod_x, part_x, spec_x,
    back_u, back_x, edge_u, edge_x,
    gather_s, gather_r, swap_s, swap_r, part_s, part_r, whole_s, whole_r,
    back_s, back_r, edge_s, edge_r, own,
):
    lat = lax.axis_index("lat")
    me = lax.axis_index("lon")
    half, turn, core = me // 8, (me // 2) % 4, me % 2
    fields = (u_ref, v_ref, q_ref)

    def count(f):
        return 8 if f == 0 else 4

    def mine(f):
        return me % 8 if f == 0 else 2 * half + core

    def lon_of(f, member):
        return 8 * half + member if f == 0 else 8 * (member // 2) + 2 * turn + member % 2

    def block(f, ref, member):
        rows = 64 // count(f)
        return ref.at[:, pl.ds(pl.multiple_of(rows * member, rows), rows)]

    def raw(f, member):
        return raw_u.at[member] if f == 0 else raw_x.at[f - 1, member]

    def back(f, member):
        return back_u.at[member] if f == 0 else back_x.at[f - 1, member]

    def edge_out(f, member):
        return edge_u.at[member] if f == 0 else edge_x.at[f - 1, member]

    def remote(src, dst, send, recv, lon, at=None):
        place = {"lon": lon} if at is None else {"lat": at, "lon": lon}
        return pltpu.make_async_remote_copy(
            src_ref=src, dst_ref=dst, send_sem=send, recv_sem=recv, device_id=place, device_id_type=MESH
        )

    def gather(f, i):
        dest = (mine(f) + i) % count(f)
        return remote(
            block(f, fields[f], dest), raw(f, mine(f)), gather_s.at[f, i], gather_r.at[f, i], lon_of(f, dest)
        )

    def own_gather(f):
        return pltpu.make_async_copy(block(f, fields[f], mine(f)), raw(f, mine(f)), own.at[f])

    def scatter(f, i):
        dest = (mine(f) + i) % count(f)
        return remote(
            back(f, dest), block(f, filt_ref.at[f], mine(f)), back_s.at[f, i], back_r.at[f, i], lon_of(f, dest)
        )

    def own_scatter(f):
        return pltpu.make_async_copy(back(f, mine(f)), block(f, filt_ref.at[f], mine(f)), own.at[3 + f])

    def swap():
        return remote(prod_u, peer_u, swap_s, swap_r, (me + 8) % 16)

    def quarter(ref, y):
        return ref.at[:, pl.ds(pl.multiple_of(32 * y, 32), 32)]

    def part(f, i):
        to = (turn + i) % 4
        return remote(
            quarter(prod_x.at[f - 1], to), part_x.at[f - 1, i - 1],
            part_s.at[f - 1, i], part_r.at[f - 1, i], 8 * half + 2 * to + core,
        )

    def whole(f, i):
        to = (turn + i) % 4
        return remote(
            quarter(spec_x.at[f - 1], turn), quarter(spec_x.at[f - 1], turn),
            whole_s.at[f - 1, i], whole_r.at[f - 1, i], 8 * half + 2 * to + core,
        )

    def edge(f, side, member):
        return remote(
            edge_out(f, member), edge_ref.at[f, side], edge_s.at[f, member], edge_r.at[f, side],
            lon_of(f, member), lat + (1 - 2 * side),
        )

    def sides(f):
        return (
            (0, jnp.logical_and(mine(f) == count(f) - 1, lat < 7), lat > 0),
            (1, jnp.logical_and(mine(f) == 0, lat > 0), lat < 7),
        )

    def each(first, last, action):
        def body(i, carry):
            action(i)
            return carry

        lax.fori_loop(first, last, body, 0)

    barrier = pltpu.get_barrier_semaphore()

    def greet(lon, at):
        pl.semaphore_signal(barrier, inc=1, device_id={"lat": at, "lon": lon}, device_id_type=MESH)

    each(1, 16, lambda i: greet((me + i) % 16, lat))

    @pl.when(lat > 0)
    def _():
        each(0, 16, lambda i: greet(i, lat - 1))

    @pl.when(lat < 7)
    def _():
        each(0, 16, lambda i: greet(i, lat + 1))

    pl.semaphore_wait(barrier, 15 + 16 * jnp.minimum(lat, 1) + 16 * jnp.minimum(7 - lat, 1))

    for f in (1, 0, 2):
        own_gather(f).start()
        each(1, count(f), lambda i, f=f: gather(f, i).start())

    for kind in range(2):
        for c in range(2):
            def fill(a, kind=kind, c=c):
                tail = jnp.where(a == 23, 1, 0)
                c1 = coarse_ref[kind, 0, pl.ds(24 * c + a, 1), :]
                s1 = coarse_ref[kind, 1, pl.ds(24 * c + a, 1), :]
                c2 = fine_ref[kind, tail, 0]
                s2 = fine_ref[kind, tail, 1]
                rows = pl.ds(pl.multiple_of(32 * a, 32), 32)
                for side, value in enumerate((c1 * c2 - s1 * s2, s1 * c2 + c1 * s2)):
                    high, low = split(value)
                    table[kind, c, rows, pl.ds(128 * side, 128)] = high
                    table[kind, c, rows, pl.ds(256 + 128 * side, 128)] = low
                    table[kind, c, rows, pl.ds(512 + 128 * side, 128)] = high

            each(0, 24, fill)
    for r in range(8):
        for c in range(2):
            y_h[c, r, :, 640:] = jnp.zeros((128, 128), BF16)
            y_l[c, r, :, 640:] = jnp.zeros((128, 128), BF16)

    row_at = lax.broadcasted_iota(jnp.int32, (8, 256), 0)
    lane_at = lax.broadcasted_iota(jnp.int32, (8, 256), 1)
    k2 = lane_at % 128
    sign = jnp.where(lane_at < 128, 1.0, -1.0).astype(F32)
    zero = jnp.where(k2 == 0, F32(0.5), F32(1.0))

    def limits_of(first):
        limits = jnp.zeros((8, 256), jnp.int32)
        for row in range(8):
            limits = jnp.where(row_at == row, cut_ref[first + row], limits)
        return limits

    def weights_of(first):
        limits = limits_of(first)

        def kept(k):
            return jnp.where(k < limits, F32(2.0 / NLON), F32(0.0))

        pairs = []
        for k1 in (1, 2, 3):
            above, below = kept(8 * k2 + 4 + k1), kept(8 * k2 + 4 - k1)
            pairs.append((above + below, (above - below) * sign))
        return kept(8 * k2 + 4), kept(8 * k2) * zero, pairs

    def keep(rows, weights):
        centre, single, pairs = weights
        out = [rows[0] * centre]
        for k1 in (1, 2, 3):
            both, odd = pairs[k1 - 1]
            r1, r2 = rows[2 * k1 - 1], rows[2 * k1]
            swap1 = jnp.concatenate([r1[:, 128:], r1[:, :128]], axis=1)
            swap2 = jnp.concatenate([r2[:, 128:], r2[:, :128]], axis=1)
            out += [both * r1 + odd * swap2, both * r2 - odd * swap1]
        return out + [rows[7] * single]

    flip = jnp.where(turn % 2 == 0, F32(1.0), F32(-1.0))

    def analyse(f, target):
        lines = 64 if f == 0 else 128
        base = 4 * half if f == 0 else turn

        def first_stage(step):
            at = pl.ds(pl.multiple_of(16 * step, 16), 16)
            for c in range(2):
                for lo in range(0, SEG, LANES):
                    hi = min(SEG, lo + LANES)
                    if f == 0:
                        x = [raw_u[2 * d + c, pl.ds(2 * step, 2), :, lo:hi].reshape(16, hi - lo) for d in range(4)]
                        s02, s13 = x[0] + x[2], x[1] + x[3]
                        minus, plus = (x[3] - x[1]) * ROOT_HALF, (x[1] + x[3]) * -ROOT_HALF
                        first, final = s02 - s13, s02 + s13
                        parts = (
                            (x[0] + minus, -x[2] - plus),
                            (x[0] - x[2], x[1] - x[3]),
                            (x[0] - minus, x[2] - plus),
                        )
                    else:
                        x0, x1 = raw_x[f - 1, c, step, :, lo:hi], raw_x[f - 1, 2 + c, step, :, lo:hi]
                        final = x0 + x1
                        first, odd = final * flip, (x0 - x1) * flip
                        parts = ((odd, None), (first, None), (odd, None))
                    rows = [first]
                    for k1, (re, im) in enumerate(parts):
                        co, si = tw_ref[base, k1, 0, c, :, lo:hi], tw_ref[base, k1, 1, c, :, lo:hi]
                        if im is None:
                            rows += [re * co, -(re * si)]
                        else:
                            rows += [re * co + im * si, im * co - re * si]
                    rows.append(final)
                    for r, value in enumerate(rows):
                        high, low = split(value)
                        y_h[c, r, at, lo:hi] = high
                        y_l[c, r, at, lo:hi] = low

        each(0, lines // 16, first_stage)
        for kind, r0, r1 in ((1, 0, 7), (0, 7, 8)):
            total = None
            for c in range(2):
                high = y_h[c, r0:r1, 0:lines, :].reshape((r1 - r0) * lines, PAD)
                low = y_l[c, r0:r1, 0:lines, :].reshape((r1 - r0) * lines, PAD)
                value = dot3(
                    high, low, table[kind, c, :, 0:256], table[kind, c, :, 256:512], ((1,), (0,))
                )
                total = value if total is None else total + value
            target[r0:r1] = total.reshape(r1 - r0, lines, 256)

    def synthesise(f, spec):
        lines = 64 if f == 0 else 128
        base = 4 * half if f == 0 else turn
        for kind, r0, r1 in ((1, 0, 7), (0, 7, 8)):
            high, low = split(spec[r0:r1].reshape((r1 - r0) * lines, 256))
            both = jnp.concatenate([high, high, low], axis=1)
            for c in range(2):
                zed[c, r0:r1, 0:lines] = lax.dot_general(
                    both, table[kind, c], (((1,), (1,)), ((), ())), preferred_element_type=F32
                ).reshape(r1 - r0, lines, PAD)

        def last_stage(step):
            at = pl.ds(pl.multiple_of(8 * step, 8), 8)
            for c in range(2):
                for lo in range(0, PAD, LANES):
                    hi = lo + LANES
                    z = [zed[c, r, at, lo:hi] for r in range(8)]
                    tw = [(tw_ref[base, k1, 0, c, :, lo:hi], tw_ref[base, k1, 1, c, :, lo:hi]) for k1 in range(3)]
                    real = [z[2 * k1 + 1] * tw[k1][0] - z[2 * k1 + 2] * tw[k1][1] for k1 in range(3)]
                    if f == 0:
                        (ar, br, cr) = real
                        ai, bi, ci = [z[2 * k1 + 2] * tw[k1][0] + z[2 * k1 + 1] * tw[k1][1] for k1 in range(3)]
                        up, down = z[0] + z[7], z[0] - z[7]
                        p, m = (ar - cr) * ROOT_HALF, (ai + ci) * ROOT_HALF
                        outs = (up + br + (ar + cr), -(down - bi + (p - m)), up - br + (ci - ai), (p + m) - (down + bi))
                        for d in range(4):
                            back_u[2 * d + c, step, :, lo:hi] = outs[d]
                    else:
                        even, odd = (z[0] + real[1]) * flip + z[7], (real[0] + real[2]) * flip
                        rows = pl.ds(pl.multiple_of(8 * (step % 2), 8), 8)
                        back_x[f - 1, c, step // 2, rows, lo:hi] = even + odd
                        back_x[f - 1, 2 + c, step // 2, rows, lo:hi] = even - odd

        each(0, lines // 8, last_stage)
        own_scatter(f).start()

    def send_edges(f):
        for side, sends, _ in sides(f):
            @pl.when(sends)
            def _(side=side):
                row = (64 // count(f) - 1) * (1 - side)
                at = 63 * (1 - side)
                factor = 1.0 / jnp.full((1, PAD), scale_ref[at], F32) if f < 2 else None

                def pack(member):
                    for level in range(8):
                        value = back(f, member)[level, row:row + 1, :]
                        edge_out(f, member)[level] = value if factor is None else value * factor

                each(0, count(f), pack)
                each(0, count(f), lambda member: edge(f, side, member).start())

    def send_back(f):
        each(1, count(f), lambda i: scatter(f, i).start())
        send_edges(f)

    def analyse_x(f):
        own_gather(f).wait()
        each(1, 4, lambda i: gather(f, i).wait_recv())
        analyse(f, prod_x.at[f - 1])
        each(1, 4, lambda i: part(f, i).start())

    def add_x(f):
        each(1, 4, lambda i: part(f, i).wait_recv())
        weights = [weights_of(16 * mine(f) + 8 * g) for g in range(2)]
        for step in range(4):
            at = pl.ds(pl.multiple_of(32 * turn + 8 * step, 8), 8)
            here = pl.ds(8 * step, 8)
            rows = []
            for r in range(8):
                value = prod_x[f - 1, r, at, :] + part_x[f - 1, 1, r, here, :]
                rows.append(value + (part_x[f - 1, 0, r, here, :] + part_x[f - 1, 2, r, here, :]))
            for r, value in enumerate(keep(rows, weights[step % 2])):
                spec_x[f - 1, r, at, :] = value
        each(1, 4, lambda i: whole(f, i).start())

    def synthesise_x(f):
        each(1, 4, lambda i: whole(f, i).wait_recv())
        synthesise(f, spec_x.at[f - 1])

    analyse_x(1)

    own_gather(0).wait()
    each(1, 8, lambda i: gather(0, i).wait_recv())
    analyse(0, prod_u)
    swap().start()

    add_x(1)
    analyse_x(2)
    synthesise_x(1)
    send_back(1)

    swap().wait_recv()
    weights = weights_of(8 * mine(0))

    def add_u(step):
        at = pl.ds(pl.multiple_of(8 * step, 8), 8)
        rows = [prod_u[r, at, :] + peer_u[r, at, :] for r in range(8)]
        for r, value in enumerate(keep(rows, weights)):
            spec_u[r, at, :] = value

    each(0, 8, add_u)
    synthesise(0, spec_u)

    add_x(2)
    send_back(0)
    synthesise_x(2)
    send_back(2)

    swap().wait_send()
    for f in (1, 0, 2):
        own_scatter(f).wait()
        if f > 0:
            each(1, 4, lambda i, f=f: part(f, i).wait_send())
            each(1, 4, lambda i, f=f: whole(f, i).wait_send())

        def finish(i, f=f):
            gather(f, i).wait_send()
            scatter(f, i).wait_send()
            scatter(f, i).wait_recv()

        each(1, count(f), finish)
        for side, sends, gets in sides(f):
            @pl.when(sends)
            def _(f=f, side=side):
                each(0, count(f), lambda member: edge(f, side, member).wait_send())

            @pl.when(gets)
            def _(f=f, side=side):
                remote(
                    edge_out(f, 0), edge_ref.at[f, side], edge_s.at[f, 0], edge_r.at[f, side], (me + 1) % 16
                ).wait_recv()


def stencil_kernel(filt_ref, edge_ref, tracer_ref, row_scale_ref, t_ref, d_ref, z_ref, scale_ref, inv_ref):
    lat = lax.axis_index("lat")

    @pl.when(pl.program_id(0) == 0)
    def _():
        def spread(row, carry):
            scale_ref[pl.ds(row, 1), :] = jnp.full((1, LANES), row_scale_ref[row], F32)
            return carry

        lax.fori_loop(0, 64, spread, 0, unroll=8)
        inv_ref[...] = 1.0 / scale_ref[...]

    scale = jnp.concatenate([scale_ref[...]] * (PAD // LANES), axis=1)
    inv = jnp.concatenate([inv_ref[...]] * (PAD // LANES), axis=1)
    first = lax.broadcasted_iota(jnp.int32, (64, PAD), 0) == 0
    last = lax.broadcasted_iota(jnp.int32, (64, PAD), 0) == 63

    def change(field, values):
        above = jnp.where(lat > 0, edge_ref[field, 0, 0], F32(0.0))
        below = jnp.where(lat < 7, edge_ref[field, 1, 0], F32(0.0))
        north = jnp.where(first, above, pltpu.roll(values, 1, 0))
        south = jnp.where(last, below, pltpu.roll(values, 63, 0))
        return south - north

    def east_west(values):
        return pltpu.roll(values, PAD - 1, 1) - pltpu.roll(values, 1, 1)

    u, v, q = filt_ref[0, 0], filt_ref[1, 0], filt_ref[2, 0]
    d_ref[0] = (scale * (east_west(u) + change(1, v * inv)))[:, :SEG]
    z_ref[0] = (scale * (east_west(v) - change(0, u * inv)))[:, :SEG]
    flux = u * scale * east_west(q) + v * change(2, q)
    t_ref[0] = tracer_ref[0] - courant * flux[:, :SEG]


def on_device(tables, wind_u, wind_v, tracer, cutoff, row_scale):
    coarse, fine, twiddle = (jnp.asarray(t) for t in tables)
    hbm = pl.BlockSpec(memory_space=pl.ANY)
    vmem = pl.BlockSpec(memory_space=pltpu.VMEM)
    smem = pl.BlockSpec(memory_space=pltpu.SMEM)
    dma = pltpu.SemaphoreType.DMA
    filt, edge = pl.pallas_call(
        filter_kernel,
        name="polar_filter",
        out_shape=(
            jax.ShapeDtypeStruct((3, 8, 64, PAD), F32),
            jax.ShapeDtypeStruct((3, 2, 8, 1, PAD), F32),
        ),
        in_specs=[hbm, hbm, hbm, smem, smem, vmem, vmem, vmem],
        out_specs=(hbm, hbm),
        scratch_shapes=[
            pltpu.VMEM((8, 8, 8, SEG), F32),
            pltpu.VMEM((2, 4, 8, 16, SEG), F32),
            pltpu.VMEM((2, 2, PAD, PAD), BF16),
            pltpu.VMEM((2, 8, 128, PAD), BF16),
            pltpu.VMEM((2, 8, 128, PAD), BF16),
            pltpu.VMEM((2, 8, 128, PAD), F32),
            pltpu.VMEM((8, 64, 256), F32),
            pltpu.VMEM((8, 64, 256), F32),
            pltpu.VMEM((8, 64, 256), F32),
            pltpu.VMEM((2, 8, 128, 256), F32),
            pltpu.VMEM((2, 3, 8, 32, 256), F32),
            pltpu.VMEM((2, 8, 128, 256), F32),
            pltpu.VMEM((8, 8, 8, PAD), F32),
            pltpu.VMEM((2, 4, 8, 16, PAD), F32),
            pltpu.VMEM((8, 8, 1, PAD), F32),
            pltpu.VMEM((2, 4, 8, 1, PAD), F32),
            dma((3, 8)), dma((3, 8)), dma, dma, dma((2, 4)), dma((2, 4)), dma((2, 4)), dma((2, 4)),
            dma((3, 8)), dma((3, 8)), dma((3, 8)), dma((3, 2)), dma((6,)),
        ],
        compiler_params=pltpu.CompilerParams(has_side_effects=True, collective_id=0, vmem_limit_bytes=60 * 1024 * 1024),
    )(wind_u, wind_v, tracer, cutoff, row_scale, coarse, fine, twiddle)
    level = pl.BlockSpec((1, 64, SEG), lambda k: (k, 0, 0))
    shape = jax.ShapeDtypeStruct((8, 64, SEG), F32)
    return pl.pallas_call(
        stencil_kernel,
        name="flux_stencil",
        grid=(8,),
        out_shape=(shape, shape, shape),
        in_specs=[
            pl.BlockSpec((3, 1, 64, PAD), lambda k: (0, k, 0, 0)),
            pl.BlockSpec((3, 2, 1, 1, PAD), lambda k: (0, 0, k, 0, 0)),
            level, smem,
        ],
        out_specs=(level, level, level),
        scratch_shapes=[pltpu.VMEM((64, LANES), F32), pltpu.VMEM((64, LANES), F32)],
    )(filt, edge, tracer, row_scale)


def solution(mesh):
    in_specs = (
        P(None, "lat", "lon"),
        P(None, "lat", "lon"),
        P(None, "lat", "lon"),
        P("lat"),
        P("lat"),
    )
    out_specs = (P(None, "lat", "lon"), P(None, "lat", "lon"), P(None, "lat", "lon"))
    return jax.shard_map(
        functools.partial(on_device, small_tables()),
        mesh=mesh, in_specs=in_specs, out_specs=out_specs, check_vma=False,
    )
```

```python
import functools
import math

import numpy as np
import jax
import jax.numpy as jnp
from jax import lax
from jax.experimental import pallas as pl
from jax.experimental.pallas import tpu as pltpu
from jax.sharding import PartitionSpec as P

NLON = 12000
SEG = 750
PAD = 768
LANES = 128
MESH = pl.DeviceIdType.MESH
F32 = jnp.float32
BF16 = jnp.bfloat16
ROOT_HALF = math.sqrt(0.5)
courant = 0.5
STREAMS = ((0, 0, 8, True, 0), (1, 0, 8, False, 0), (2, 0, 6, False, 0), (2, 6, 2, True, 8))


def phase(steps):
    angle = 2.0 * np.pi * (np.asarray(steps, dtype=np.int64) % NLON) / NLON
    return np.stack([np.cos(angle), np.sin(angle)]).astype(np.float32)


def small_tables():
    k2 = np.arange(128)
    start = (750 * np.arange(2)[:, None] + 32 * np.arange(24)[None, :]).reshape(48)
    inner = np.arange(32)
    last = np.where(inner == 31, -1 - 736, inner)
    coarse, fine = [], []
    for mult in (8 * k2, 8 * k2 + 4):
        coarse.append(phase(start[:, None] * mult[None, :]))
        fine.append(np.stack([phase(b[:, None] * mult[None, :]) for b in (inner, last)]))
    lanes = np.arange(PAD)
    lanes = np.where(lanes == PAD - 1, -1, lanes)
    place = 750 * np.arange(2)[:, None] + lanes[None, :]
    twiddle = np.stack([np.stack([phase(k1 * (1500 * d + place)) for k1 in (1, 2, 3)]) for d in range(8)])
    return np.stack(coarse), np.stack(fine), twiddle[:, :, :, :, None, :]


def split(values):
    high = values.astype(BF16)
    return high, (values - high.astype(F32)).astype(BF16)


def dot3(high, low, table_high, table_low, dims):
    def one(a, b):
        return lax.dot_general(a, b, (dims, ((), ())), preferred_element_type=F32)

    return one(high, table_high) + (one(high, table_low) + one(low, table_high))


def filter_kernel(
    u_ref, v_ref, q_ref, cut_ref, scale_ref, coarse_ref, fine_ref, tw_ref,
    filt_ref, edge_ref,
    raw_u, raw_x, table, y_h, y_l, zed,
    prod_u, peer_u, spec_u, prod_x, part_x, relay_x, spec_x,
    back_u, back_x, edge_u, edge_x,
    gather_s, gather_r, swap_s, swap_r, part_s, part_r, whole_s, whole_r,
    back_s, back_r, edge_s, edge_r, own,
):
    lat = lax.axis_index("lat")
    me = lax.axis_index("lon")
    half, turn, core = me // 8, (me // 2) % 4, me % 2
    fields = (u_ref, v_ref, q_ref)

    def column(f):
        return STREAMS[f][3]

    def count(f):
        return 8 if column(f) else 4

    def mine(f):
        return me % 8 if column(f) else 2 * half + core

    def lon_of(f, member):
        return 8 * half + member if column(f) else 8 * (member // 2) + 2 * turn + member % 2

    def levels(f):
        return pl.ds(STREAMS[f][1], STREAMS[f][2])

    def place(f):
        return pl.ds(STREAMS[f][4], STREAMS[f][2])

    def block(f, ref, member):
        rows = 64 // count(f)
        return ref.at[levels(f), pl.ds(pl.multiple_of(rows * member, rows), rows)]

    def source(f):
        return fields[STREAMS[f][0]]

    def result(f):
        return filt_ref.at[STREAMS[f][0]]

    def raw(f, member):
        return raw_u.at[member, place(f)] if column(f) else raw_x.at[f - 1, member, place(f)]

    def back(f, member):
        return back_u.at[member, place(f)] if column(f) else back_x.at[f - 1, member, place(f)]

    def edge_out(f, member):
        return edge_u.at[member, place(f)] if column(f) else edge_x.at[f - 1, member, place(f)]

    def remote(src, dst, send, recv, lon, at=None):
        place = {"lon": lon} if at is None else {"lat": at, "lon": lon}
        return pltpu.make_async_remote_copy(
            src_ref=src, dst_ref=dst, send_sem=send, recv_sem=recv, device_id=place, device_id_type=MESH
        )

    def gather(f, i):
        dest = (mine(f) + i) % count(f)
        return remote(
            block(f, source(f), dest), raw(f, mine(f)), gather_s.at[f, i], gather_r.at[f, i], lon_of(f, dest)
        )

    def own_gather(f):
        return pltpu.make_async_copy(block(f, source(f), mine(f)), raw(f, mine(f)), own.at[f])

    def scatter(f, i):
        dest = (mine(f) + i) % count(f)
        return remote(
            back(f, dest), block(f, result(f), mine(f)), back_s.at[f, i], back_r.at[f, i], lon_of(f, dest)
        )

    def own_scatter(f):
        return pltpu.make_async_copy(back(f, mine(f)), block(f, result(f), mine(f)), own.at[4 + f])

    def swap():
        return remote(prod_u, peer_u, swap_s, swap_r, (me + 8) % 16)

    odd_turn = turn % 2
    near = (turn + 1 - 2 * odd_turn, (turn + 3 + 2 * odd_turn) % 4)
    opposite = (turn + 2) % 4

    def size(f):
        return 4 * STREAMS[f][2]

    def quarter(f, ref, y, rows):
        return ref.at[f - 1, rows, pl.ds(pl.multiple_of(size(f) * y, 8), size(f))]

    def four(d):
        return pl.ds(4 * d, 4)

    def beside(d):
        return 8 * half + 2 * near[d] + core

    def part(f, d, slot):
        if slot == 2:
            src = relay_x.at[f - 1, d, :, pl.ds(0, size(f))]
        else:
            src = quarter(f, prod_x, near[d] if slot == 0 else opposite, four(d))
        return remote(
            src, part_x.at[f - 1, d, slot, :, pl.ds(0, size(f))],
            part_s.at[f - 1, d, slot], part_r.at[f - 1, d, slot], beside(d),
        )

    def whole(f, d, slot):
        if slot == 0:
            piece = quarter(f, spec_x, turn, pl.ds(0, 8))
        else:
            piece = quarter(f, spec_x, near[1 - d], four(d))
        return remote(piece, piece, whole_s.at[f - 1, d, slot], whole_r.at[f - 1, d, slot], beside(d))

    def whole_arrival(f, d, slot):
        if slot == 0:
            piece = quarter(f, spec_x, near[d], pl.ds(0, 8))
        else:
            piece = quarter(f, spec_x, opposite, four(d))
        return remote(piece, piece, whole_s.at[f - 1, d, slot], whole_r.at[f - 1, d, slot], beside(d))

    def edge(f, side, member):
        return remote(
            edge_out(f, member), edge_ref.at[STREAMS[f][0], side, levels(f)], edge_s.at[f, member], edge_r.at[f, side],
            lon_of(f, member), lat + (1 - 2 * side),
        )

    def sides(f):
        return (
            (0, jnp.logical_and(mine(f) == count(f) - 1, lat < 7), lat > 0),
            (1, jnp.logical_and(mine(f) == 0, lat > 0), lat < 7),
        )

    def each(first, last, action):
        def body(i, carry):
            action(i)
            return carry

        lax.fori_loop(first, last, body, 0)

    barrier = pltpu.get_barrier_semaphore()

    def greet(lon, at):
        pl.semaphore_signal(barrier, inc=1, device_id={"lat": at, "lon": lon}, device_id_type=MESH)

    each(1, 8, lambda i: greet(8 * half + (me + i) % 8, lat))
    for other in (core, 1 - core):
        greet(8 * (1 - half) + 2 * turn + other, lat)

    @pl.when(lat > 0)
    def _():
        greet(8 * half + 7, lat - 1)
        greet(2 * turn + 9, lat - 1)

    @pl.when(lat < 7)
    def _():
        greet(8 * half, lat + 1)
        greet(2 * turn, lat + 1)

    def either(yes):
        return jnp.where(yes, 1, 0)

    lower = 8 * either(me % 8 == 7) + 4 * either(half + core == 2)
    upper = 8 * either(me % 8 == 0) + 4 * either(half + core == 0)
    pl.semaphore_wait(barrier, 9 + lower * either(lat < 7) + upper * either(lat > 0))

    for f in (1, 0, 3, 2):
        own_gather(f).start()
        each(1, count(f), lambda i, f=f: gather(f, i).start())

    for kind in range(2):
        for c in range(2):
            def fill(a, kind=kind, c=c):
                tail = jnp.where(a == 23, 1, 0)
                c1 = coarse_ref[kind, 0, pl.ds(24 * c + a, 1), :]
                s1 = coarse_ref[kind, 1, pl.ds(24 * c + a, 1), :]
                c2 = fine_ref[kind, tail, 0]
                s2 = fine_ref[kind, tail, 1]
                rows = pl.ds(pl.multiple_of(32 * a, 32), 32)
                for side, value in enumerate((c1 * c2 - s1 * s2, s1 * c2 + c1 * s2)):
                    high, low = split(value)
                    table[kind, c, rows, pl.ds(128 * side, 128)] = high
                    table[kind, c, rows, pl.ds(256 + 128 * side, 128)] = low
                    table[kind, c, rows, pl.ds(512 + 128 * side, 128)] = high

            each(0, 24, fill)
    for r in range(8):
        for c in range(2):
            y_h[c, r, :, 640:] = jnp.zeros((128, 128), BF16)
            y_l[c, r, :, 640:] = jnp.zeros((128, 128), BF16)

    row_at = lax.broadcasted_iota(jnp.int32, (8, 256), 0)
    lane_at = lax.broadcasted_iota(jnp.int32, (8, 256), 1)
    k2 = lane_at % 128
    sign = jnp.where(lane_at < 128, 1.0, -1.0).astype(F32)
    zero = jnp.where(k2 == 0, F32(0.5), F32(1.0))

    def limits_of(first):
        limits = jnp.zeros((8, 256), jnp.int32)
        for row in range(8):
            limits = jnp.where(row_at == row, cut_ref[first + row], limits)
        return limits

    def weights_of(first):
        limits = limits_of(first)

        def kept(k):
            return jnp.where(k < limits, F32(2.0 / NLON), F32(0.0))

        pairs = []
        for k1 in (1, 2, 3):
            above, below = kept(8 * k2 + 4 + k1), kept(8 * k2 + 4 - k1)
            pairs.append((above + below, (above - below) * sign))
        return kept(8 * k2 + 4), kept(8 * k2) * zero, pairs

    def keep(rows, weights):
        centre, single, pairs = weights
        out = [rows[0] * centre]
        for k1 in (1, 2, 3):
            both, odd = pairs[k1 - 1]
            r1, r2 = rows[2 * k1 - 1], rows[2 * k1]
            swap1 = jnp.concatenate([r1[:, 128:], r1[:, :128]], axis=1)
            swap2 = jnp.concatenate([r2[:, 128:], r2[:, :128]], axis=1)
            out += [both * r1 + odd * swap2, both * r2 - odd * swap1]
        return out + [rows[7] * single]

    flip = jnp.where(turn % 2 == 0, F32(1.0), F32(-1.0))

    def analyse(f, target):
        lines = 80 if column(f) else 16 * STREAMS[f][2]
        base = 4 * half if column(f) else turn

        def first_stage(step):
            at = pl.ds(pl.multiple_of(16 * step, 16), 16)
            for c in range(2):
                for lo in range(0, SEG, LANES):
                    hi = min(SEG, lo + LANES)
                    if column(f):
                        x = [raw_u[2 * d + c, pl.ds(2 * step, 2), :, lo:hi].reshape(16, hi - lo) for d in range(4)]
                        s02, s13 = x[0] + x[2], x[1] + x[3]
                        minus, plus = (x[3] - x[1]) * ROOT_HALF, (x[1] + x[3]) * -ROOT_HALF
                        first, final = s02 - s13, s02 + s13
                        parts = (
                            (x[0] + minus, -x[2] - plus),
                            (x[0] - x[2], x[1] - x[3]),
                            (x[0] - minus, x[2] - plus),
                        )
                    else:
                        x0, x1 = raw_x[f - 1, c, step, :, lo:hi], raw_x[f - 1, 2 + c, step, :, lo:hi]
                        final = x0 + x1
                        first, odd = final * flip, (x0 - x1) * flip
                        parts = ((odd, None), (first, None), (odd, None))
                    rows = [first]
                    for k1, (re, im) in enumerate(parts):
                        co, si = tw_ref[base, k1, 0, c, :, lo:hi], tw_ref[base, k1, 1, c, :, lo:hi]
                        if im is None:
                            rows += [re * co, -(re * si)]
                        else:
                            rows += [re * co + im * si, im * co - re * si]
                    rows.append(final)
                    for r, value in enumerate(rows):
                        high, low = split(value)
                        y_h[c, r, at, lo:hi] = high
                        y_l[c, r, at, lo:hi] = low

        each(0, lines // 16, first_stage)
        for kind, r0, r1 in ((1, 0, 7), (0, 7, 8)):
            total = None
            for c in range(2):
                high = y_h[c, r0:r1, 0:lines, :].reshape((r1 - r0) * lines, PAD)
                low = y_l[c, r0:r1, 0:lines, :].reshape((r1 - r0) * lines, PAD)
                value = dot3(
                    high, low, table[kind, c, :, 0:256], table[kind, c, :, 256:512], ((1,), (0,))
                )
                total = value if total is None else total + value
            target[r0:r1, 0:lines] = total.reshape(r1 - r0, lines, 256)

    def synthesise(f, spec):
        lines = 80 if column(f) else 16 * STREAMS[f][2]
        base = 4 * half if column(f) else turn
        for kind, r0, r1 in ((1, 0, 7), (0, 7, 8)):
            high, low = split(spec[r0:r1, 0:lines].reshape((r1 - r0) * lines, 256))
            both = jnp.concatenate([high, high, low], axis=1)
            for c in range(2):
                zed[c, r0:r1, 0:lines] = lax.dot_general(
                    both, table[kind, c], (((1,), (1,)), ((), ())), preferred_element_type=F32
                ).reshape(r1 - r0, lines, PAD)

        def last_stage(step):
            at = pl.ds(pl.multiple_of(8 * step, 8), 8)
            for c in range(2):
                for lo in range(0, PAD, LANES):
                    hi = lo + LANES
                    z = [zed[c, r, at, lo:hi] for r in range(8)]
                    tw = [(tw_ref[base, k1, 0, c, :, lo:hi], tw_ref[base, k1, 1, c, :, lo:hi]) for k1 in range(3)]
                    real = [z[2 * k1 + 1] * tw[k1][0] - z[2 * k1 + 2] * tw[k1][1] for k1 in range(3)]
                    if column(f):
                        (ar, br, cr) = real
                        ai, bi, ci = [z[2 * k1 + 2] * tw[k1][0] + z[2 * k1 + 1] * tw[k1][1] for k1 in range(3)]
                        up, down = z[0] + z[7], z[0] - z[7]
                        p, m = (ar - cr) * ROOT_HALF, (ai + ci) * ROOT_HALF
                        outs = (up + br + (ar + cr), -(down - bi + (p - m)), up - br + (ci - ai), (p + m) - (down + bi))
                        for d in range(4):
                            back_u[2 * d + c, step, :, lo:hi] = outs[d]
                    else:
                        even, odd = (z[0] + real[1]) * flip + z[7], (real[0] + real[2]) * flip
                        rows = pl.ds(pl.multiple_of(8 * (step % 2), 8), 8)
                        back_x[f - 1, c, step // 2, rows, lo:hi] = even + odd
                        back_x[f - 1, 2 + c, step // 2, rows, lo:hi] = even - odd

        each(0, lines // 8, last_stage)

    def send_edges(f):
        for side, sends, _ in sides(f):
            @pl.when(sends)
            def _(side=side):
                row = (64 // count(f) - 1) * (1 - side)
                at = 63 * (1 - side)
                factor = 1.0 / jnp.full((1, PAD), scale_ref[at], F32) if STREAMS[f][0] < 2 else None

                def pack(member):
                    for level in range(STREAMS[f][2]):
                        value = back(f, member)[level, row:row + 1, :]
                        edge_out(f, member)[level] = value if factor is None else value * factor

                each(0, count(f), pack)
                each(0, count(f), lambda member: edge(f, side, member).start())

    def send_back(f):
        own_scatter(f).start()
        each(1, count(f), lambda i: scatter(f, i).start())
        send_edges(f)

    def arrive(f):
        own_gather(f).wait()
        each(1, count(f), lambda i: gather(f, i).wait_recv())

    def analyse_x(f):
        arrive(f)
        analyse(f, prod_x.at[f - 1])
        for slot in (1, 0):
            for d in range(2):
                part(f, d, slot).start()

    def relay(f):
        for d in range(2):
            part(f, 1 - d, 1).wait_recv()
            at = pl.ds(pl.multiple_of(size(f) * near[d], 8), size(f))
            relay_x[f - 1, d, :, 0:size(f), :] = (
                prod_x[f - 1, 4 - 4 * d:8 - 4 * d, at, :] + part_x[f - 1, 1 - d, 1, :, 0:size(f), :]
            )
            part(f, d, 2).start()

    def add_x(f):
        for d in range(2):
            part(f, d, 0).wait_recv()
            part(f, d, 2).wait_recv()
        groups = size(f) // 8
        weights = [weights_of(16 * mine(f) + 8 * ((groups * turn + g) % 2)) for g in range(2)]
        for step in range(groups):
            at = pl.ds(pl.multiple_of(size(f) * turn + 8 * step, 8), 8)
            here = pl.ds(8 * step, 8)
            rows = []
            for r in range(8):
                d = r // 4
                value = prod_x[f - 1, r, at, :] + part_x[f - 1, d, 0, r % 4, here, :]
                rows.append(value + part_x[f - 1, 1 - d, 2, r % 4, here, :])
            for r, value in enumerate(keep(rows, weights[step % 2])):
                spec_x[f - 1, r, at, :] = value
        for d in range(2):
            whole(f, d, 0).start()

    def spread(f):
        for d in range(2):
            whole_arrival(f, d, 0).wait_recv()
        for d in range(2):
            whole(f, d, 1).start()

    def synthesise_x(f):
        for d in range(2):
            whole_arrival(f, d, 1).wait_recv()
        synthesise(f, spec_x.at[f - 1])

    analyse_x(1)
    arrive(0)
    arrive(3)
    analyse(0, prod_u)
    swap().start()
    relay(1)
    add_x(1)
    analyse_x(2)
    spread(1)
    relay(2)
    synthesise_x(1)
    send_back(1)
    add_x(2)

    swap().wait_recv()
    weights = weights_of(8 * mine(0))

    def add_u(step):
        at = pl.ds(pl.multiple_of(8 * step, 8), 8)
        rows = [prod_u[r, at, :] + peer_u[r, at, :] for r in range(8)]
        for r, value in enumerate(keep(rows, weights)):
            spec_u[r, at, :] = value

    each(0, 10, add_u)
    spread(2)
    synthesise(0, spec_u)
    send_back(0)
    send_back(3)
    synthesise_x(2)
    send_back(2)

    swap().wait_send()
    for f in (1, 0, 3, 2):
        own_scatter(f).wait()
        if not column(f):
            for d in range(2):
                for slot in range(3):
                    part(f, d, slot).wait_send()
                for slot in range(2):
                    whole(f, d, slot).wait_send()

        def finish(i, f=f):
            gather(f, i).wait_send()
            scatter(f, i).wait_send()
            scatter(f, i).wait_recv()

        each(1, count(f), finish)
        for side, sends, gets in sides(f):
            @pl.when(sends)
            def _(f=f, side=side):
                each(0, count(f), lambda member: edge(f, side, member).wait_send())

            @pl.when(gets)
            def _(f=f, side=side):
                remote(
                    edge_out(f, 0), edge_ref.at[STREAMS[f][0], side, levels(f)],
                    edge_s.at[f, 0], edge_r.at[f, side], (me + 1) % 16,
                ).wait_recv()


def stencil_kernel(filt_ref, edge_ref, tracer_ref, row_scale_ref, t_ref, d_ref, z_ref, scale_ref, inv_ref):
    lat = lax.axis_index("lat")

    @pl.when(pl.program_id(0) == 0)
    def _():
        def spread(row, carry):
            scale_ref[pl.ds(row, 1), :] = jnp.full((1, LANES), row_scale_ref[row], F32)
            return carry

        lax.fori_loop(0, 64, spread, 0, unroll=8)
        inv_ref[...] = 1.0 / scale_ref[...]

    first = lax.broadcasted_iota(jnp.int32, (64, LANES), 0) == 0
    last = lax.broadcasted_iota(jnp.int32, (64, LANES), 0) == 63
    lane = lax.broadcasted_iota(jnp.int32, (64, LANES), 1)

    def one_level(level, carry):
        for lo in range(0, PAD, LANES):
            hi, width = lo + LANES, min(LANES, SEG - lo)
            east, west = hi % PAD, (lo - LANES) % PAD

            def change(field, values):
                above = jnp.where(lat > 0, edge_ref[field, 0, level, :, lo:hi], F32(0.0))
                below = jnp.where(lat < 7, edge_ref[field, 1, level, :, lo:hi], F32(0.0))
                north = jnp.where(first, above, pltpu.roll(values, 1, 0))
                south = jnp.where(last, below, pltpu.roll(values, 63, 0))
                return south - north

            def east_west(field, values):
                right = jnp.where(lane == 0, filt_ref[field, level, :, east:east + LANES], values)
                left = jnp.where(lane == LANES - 1, filt_ref[field, level, :, west:west + LANES], values)
                return pltpu.roll(right, LANES - 1, 1) - pltpu.roll(left, 1, 1)

            u, v, q = (filt_ref[field, level, :, lo:hi] for field in range(3))
            scale, inv = scale_ref[...], inv_ref[...]
            d_ref[level, :, lo:lo + width] = (scale * (east_west(0, u) + change(1, v * inv)))[:, :width]
            z_ref[level, :, lo:lo + width] = (scale * (east_west(1, v) - change(0, u * inv)))[:, :width]
            flux = u * scale * east_west(2, q) + v * change(2, q)
            t_ref[level, :, lo:lo + width] = tracer_ref[level, :, lo:lo + width] - courant * flux[:, :width]
        return carry

    lax.fori_loop(0, 4, one_level, 0)


def on_device(tables, wind_u, wind_v, tracer, cutoff, row_scale):
    coarse, fine, twiddle = (jnp.asarray(t) for t in tables)
    hbm = pl.BlockSpec(memory_space=pl.ANY)
    vmem = pl.BlockSpec(memory_space=pltpu.VMEM)
    smem = pl.BlockSpec(memory_space=pltpu.SMEM)
    dma = pltpu.SemaphoreType.DMA
    filt, edge = pl.pallas_call(
        filter_kernel,
        name="polar_filter",
        out_shape=(
            jax.ShapeDtypeStruct((3, 8, 64, PAD), F32),
            jax.ShapeDtypeStruct((3, 2, 8, 1, PAD), F32),
        ),
        in_specs=[hbm, hbm, hbm, smem, smem, vmem, vmem, vmem],
        out_specs=(hbm, hbm),
        scratch_shapes=[
            pltpu.VMEM((8, 10, 8, SEG), F32),
            pltpu.VMEM((2, 4, 8, 16, SEG), F32),
            pltpu.VMEM((2, 2, PAD, PAD), BF16),
            pltpu.VMEM((2, 8, 128, PAD), BF16),
            pltpu.VMEM((2, 8, 128, PAD), BF16),
            pltpu.VMEM((2, 8, 128, PAD), F32),
            pltpu.VMEM((8, 80, 256), F32),
            pltpu.VMEM((8, 80, 256), F32),
            pltpu.VMEM((8, 80, 256), F32),
            pltpu.VMEM((2, 8, 128, 256), F32),
            pltpu.VMEM((2, 2, 3, 4, 32, 256), F32),
            pltpu.VMEM((2, 2, 4, 32, 256), F32),
            pltpu.VMEM((2, 8, 128, 256), F32),
            pltpu.VMEM((8, 10, 8, PAD), F32),
            pltpu.VMEM((2, 4, 8, 16, PAD), F32),
            pltpu.VMEM((8, 10, 1, PAD), F32),
            pltpu.VMEM((2, 4, 8, 1, PAD), F32),
            dma((4, 8)), dma((4, 8)), dma, dma, dma((2, 2, 3)), dma((2, 2, 3)), dma((2, 2, 2)), dma((2, 2, 2)),
            dma((4, 8)), dma((4, 8)), dma((4, 8)), dma((4, 2)), dma((8,)),
        ],
        compiler_params=pltpu.CompilerParams(has_side_effects=True, collective_id=0, vmem_limit_bytes=60 * 1024 * 1024),
    )(wind_u, wind_v, tracer, cutoff, row_scale, coarse, fine, twiddle)
    level = pl.BlockSpec((4, 64, SEG), lambda k: (k, 0, 0))
    shape = jax.ShapeDtypeStruct((8, 64, SEG), F32)
    return pl.pallas_call(
        stencil_kernel,
        name="flux_stencil",
        grid=(2,),
        out_shape=(shape, shape, shape),
        in_specs=[
            pl.BlockSpec((3, 4, 64, PAD), lambda k: (0, k, 0, 0)),
            pl.BlockSpec((3, 2, 4, 1, PAD), lambda k: (0, 0, k, 0, 0)),
            level, smem,
        ],
        out_specs=(level, level, level),
        scratch_shapes=[pltpu.VMEM((64, LANES), F32), pltpu.VMEM((64, LANES), F32)],
    )(filt, edge, tracer, row_scale)


def solution(mesh):
    in_specs = (
        P(None, "lat", "lon"),
        P(None, "lat", "lon"),
        P(None, "lat", "lon"),
        P("lat"),
        P("lat"),
    )
    out_specs = (P(None, "lat", "lon"), P(None, "lat", "lon"), P(None, "lat", "lon"))
    return jax.shard_map(
        functools.partial(on_device, small_tables()),
        mesh=mesh, in_specs=in_specs, out_specs=out_specs, check_vma=False,
    )
```

```python
import functools
import math

import numpy as np
import jax
import jax.numpy as jnp
from jax import lax
from jax.experimental import pallas as pl
from jax.experimental.pallas import tpu as pltpu
from jax.sharding import PartitionSpec as P

NLON = 12000
SEG = 750
PAD = 768
LANES = 128
MESH = pl.DeviceIdType.MESH
F32 = jnp.float32
BF16 = jnp.bfloat16
ROOT_HALF = math.sqrt(0.5)
courant = 0.5
STREAMS = ((0, 0, 8, True, 0), (1, 0, 8, False, 0), (2, 0, 6, False, 0), (2, 6, 2, True, 8))


def phase(steps):
    angle = 2.0 * np.pi * (np.asarray(steps, dtype=np.int64) % NLON) / NLON
    return np.stack([np.cos(angle), np.sin(angle)]).astype(np.float32)


def small_tables():
    k2 = np.arange(128)
    start = (750 * np.arange(2)[:, None] + 32 * np.arange(24)[None, :]).reshape(48)
    inner = np.arange(32)
    last = np.where(inner == 31, -1 - 736, inner)
    coarse, fine = [], []
    for mult in (8 * k2, 8 * k2 + 4):
        coarse.append(phase(start[:, None] * mult[None, :]))
        fine.append(np.stack([phase(b[:, None] * mult[None, :]) for b in (inner, last)]))
    lanes = np.arange(PAD)
    lanes = np.where(lanes == PAD - 1, -1, lanes)
    place = 750 * np.arange(2)[:, None] + lanes[None, :]
    twiddle = np.stack([np.stack([phase(k1 * (1500 * d + place)) for k1 in (1, 2, 3)]) for d in range(8)])
    return np.stack(coarse), np.stack(fine), twiddle[:, :, :, :, None, :]


def split(values):
    high = values.astype(BF16)
    return high, (values - high.astype(F32)).astype(BF16)


def dot3(high, low, table_high, table_low, dims):
    def one(a, b):
        return lax.dot_general(a, b, (dims, ((), ())), preferred_element_type=F32)

    return one(high, table_high) + (one(high, table_low) + one(low, table_high))


def filter_kernel(
    u_ref, v_ref, q_ref, cut_ref, scale_ref, coarse_far, fine_far, tw_far,
    filt_ref, edge_ref,
    raw_u, raw_x, table, y_h, y_l, zed,
    prod_u, peer_u, spec_u, prod_x, part_x, relay_x, spec_x,
    back_u, back_x, edge_u, edge_x,
    coarse_ref, fine_ref, tw_ref, seed_s,
    gather_s, gather_r, swap_s, swap_r, part_s, part_r, whole_s, whole_r,
    back_s, back_r, edge_s, edge_r, own,
):
    lat = lax.axis_index("lat")
    me = lax.axis_index("lon")
    half, turn, core = me // 8, (me // 2) % 4, me % 2
    fields = (u_ref, v_ref, q_ref)

    def column(f):
        return STREAMS[f][3]

    def count(f):
        return 8 if column(f) else 4

    def mine(f):
        return me % 8 if column(f) else 2 * half + core

    def lon_of(f, member):
        return 8 * half + member if column(f) else 8 * (member // 2) + 2 * turn + member % 2

    def levels(f):
        return pl.ds(STREAMS[f][1], STREAMS[f][2])

    def place(f):
        return pl.ds(STREAMS[f][4], STREAMS[f][2])

    def block(f, ref, member):
        rows = 64 // count(f)
        return ref.at[levels(f), pl.ds(pl.multiple_of(rows * member, rows), rows)]

    def source(f):
        return fields[STREAMS[f][0]]

    def result(f):
        return filt_ref.at[STREAMS[f][0]]

    def raw(f, member):
        return raw_u.at[member, place(f)] if column(f) else raw_x.at[f - 1, member, place(f)]

    def back(f, member):
        return back_u.at[member, place(f)] if column(f) else back_x.at[f - 1, member, place(f)]

    def edge_out(f, member):
        return edge_u.at[member, place(f)] if column(f) else edge_x.at[f - 1, member, place(f)]

    def remote(src, dst, send, recv, lon, at=None):
        place = {"lon": lon} if at is None else {"lat": at, "lon": lon}
        return pltpu.make_async_remote_copy(
            src_ref=src, dst_ref=dst, send_sem=send, recv_sem=recv, device_id=place, device_id_type=MESH
        )

    def gather(f, i):
        dest = (mine(f) + i) % count(f)
        return remote(
            block(f, source(f), dest), raw(f, mine(f)), gather_s.at[f, i], gather_r.at[f, i], lon_of(f, dest)
        )

    def own_gather(f):
        return pltpu.make_async_copy(block(f, source(f), mine(f)), raw(f, mine(f)), own.at[f])

    def scatter(f, i):
        dest = (mine(f) + i) % count(f)
        return remote(
            back(f, dest), block(f, result(f), mine(f)), back_s.at[f, i], back_r.at[f, i], lon_of(f, dest)
        )

    def own_scatter(f):
        return pltpu.make_async_copy(back(f, mine(f)), block(f, result(f), mine(f)), own.at[4 + f])

    def swap():
        return remote(prod_u, peer_u, swap_s, swap_r, (me + 8) % 16)

    odd_turn = turn % 2
    near = (turn + 1 - 2 * odd_turn, (turn + 3 + 2 * odd_turn) % 4)
    opposite = (turn + 2) % 4

    def size(f):
        return 4 * STREAMS[f][2]

    def quarter(f, ref, y, rows):
        return ref.at[f - 1, rows, pl.ds(pl.multiple_of(size(f) * y, 8), size(f))]

    def four(d):
        return pl.ds(4 * d, 4)

    def beside(d):
        return 8 * half + 2 * near[d] + core

    def part(f, d, slot):
        if slot == 2:
            src = relay_x.at[f - 1, d, :, pl.ds(0, size(f))]
        else:
            src = quarter(f, prod_x, near[d] if slot == 0 else opposite, four(d))
        return remote(
            src, part_x.at[f - 1, d, slot, :, pl.ds(0, size(f))],
            part_s.at[f - 1, d, slot], part_r.at[f - 1, d, slot], beside(d),
        )

    def whole(f, d, slot):
        if slot == 0:
            piece = quarter(f, spec_x, turn, pl.ds(0, 8))
        else:
            piece = quarter(f, spec_x, near[1 - d], four(d))
        return remote(piece, piece, whole_s.at[f - 1, d, slot], whole_r.at[f - 1, d, slot], beside(d))

    def whole_arrival(f, d, slot):
        if slot == 0:
            piece = quarter(f, spec_x, near[d], pl.ds(0, 8))
        else:
            piece = quarter(f, spec_x, opposite, four(d))
        return remote(piece, piece, whole_s.at[f - 1, d, slot], whole_r.at[f - 1, d, slot], beside(d))

    def edge(f, side, member):
        return remote(
            edge_out(f, member), edge_ref.at[STREAMS[f][0], side, levels(f)], edge_s.at[f, member], edge_r.at[f, side],
            lon_of(f, member), lat + (1 - 2 * side),
        )

    def sides(f):
        return (
            (0, jnp.logical_and(mine(f) == count(f) - 1, lat < 7), lat > 0),
            (1, jnp.logical_and(mine(f) == 0, lat > 0), lat < 7),
        )

    def each(first, last, action):
        def body(i, carry):
            action(i)
            return carry

        lax.fori_loop(first, last, body, 0)

    barrier = pltpu.get_barrier_semaphore()

    def greet(lon, at):
        pl.semaphore_signal(barrier, inc=1, device_id={"lat": at, "lon": lon}, device_id_type=MESH)

    each(1, 8, lambda i: greet(8 * half + (me + i) % 8, lat))
    for other in (core, 1 - core):
        greet(8 * (1 - half) + 2 * turn + other, lat)

    @pl.when(lat > 0)
    def _():
        greet(8 * half + 7, lat - 1)
        greet(2 * turn + 9, lat - 1)

    @pl.when(lat < 7)
    def _():
        greet(8 * half, lat + 1)
        greet(2 * turn, lat + 1)

    def either(yes):
        return jnp.where(yes, 1, 0)

    lower = 8 * either(me % 8 == 7) + 4 * either(half + core == 2)
    upper = 8 * either(me % 8 == 0) + 4 * either(half + core == 0)
    pl.semaphore_wait(barrier, 9 + lower * either(lat < 7) + upper * either(lat > 0))

    for f in (1, 0, 3, 2):
        own_gather(f).start()
        each(1, count(f), lambda i, f=f: gather(f, i).start())

    seeds = (
        pltpu.make_async_copy(coarse_far, coarse_ref, seed_s.at[0]),
        pltpu.make_async_copy(fine_far, fine_ref, seed_s.at[1]),
        pltpu.make_async_copy(tw_far.at[turn], tw_ref.at[0], seed_s.at[2]),
        pltpu.make_async_copy(tw_far.at[4 * half], tw_ref.at[1], seed_s.at[3]),
    )
    for seed in seeds:
        seed.start()
    for seed in seeds:
        seed.wait()

    for kind in range(2):
        for c in range(2):
            def fill(a, kind=kind, c=c):
                tail = jnp.where(a == 23, 1, 0)
                c1 = coarse_ref[kind, 0, pl.ds(24 * c + a, 1), :]
                s1 = coarse_ref[kind, 1, pl.ds(24 * c + a, 1), :]
                c2 = fine_ref[kind, tail, 0]
                s2 = fine_ref[kind, tail, 1]
                rows = pl.ds(pl.multiple_of(32 * a, 32), 32)
                for side, value in enumerate((c1 * c2 - s1 * s2, s1 * c2 + c1 * s2)):
                    high, low = split(value)
                    table[kind, c, rows, pl.ds(128 * side, 128)] = high
                    table[kind, c, rows, pl.ds(256 + 128 * side, 128)] = low
                    table[kind, c, rows, pl.ds(512 + 128 * side, 128)] = high

            each(0, 24, fill)
    for r in range(8):
        for c in range(2):
            y_h[c, r, :, 640:] = jnp.zeros((128, 128), BF16)
            y_l[c, r, :, 640:] = jnp.zeros((128, 128), BF16)

    row_at = lax.broadcasted_iota(jnp.int32, (8, 256), 0)
    lane_at = lax.broadcasted_iota(jnp.int32, (8, 256), 1)
    k2 = lane_at % 128
    sign = jnp.where(lane_at < 128, 1.0, -1.0).astype(F32)
    zero = jnp.where(k2 == 0, F32(0.5), F32(1.0))

    def limits_of(first):
        limits = jnp.zeros((8, 256), jnp.int32)
        for row in range(8):
            limits = jnp.where(row_at == row, cut_ref[first + row], limits)
        return limits

    def weights_of(first):
        limits = limits_of(first)

        def kept(k):
            return jnp.where(k < limits, F32(2.0 / NLON), F32(0.0))

        pairs = []
        for k1 in (1, 2, 3):
            above, below = kept(8 * k2 + 4 + k1), kept(8 * k2 + 4 - k1)
            pairs.append((above + below, (above - below) * sign))
        return kept(8 * k2 + 4), kept(8 * k2) * zero, pairs

    def keep(rows, weights):
        centre, single, pairs = weights
        out = [rows[0] * centre]
        for k1 in (1, 2, 3):
            both, odd = pairs[k1 - 1]
            r1, r2 = rows[2 * k1 - 1], rows[2 * k1]
            swap1 = jnp.concatenate([r1[:, 128:], r1[:, :128]], axis=1)
            swap2 = jnp.concatenate([r2[:, 128:], r2[:, :128]], axis=1)
            out += [both * r1 + odd * swap2, both * r2 - odd * swap1]
        return out + [rows[7] * single]

    flip = jnp.where(turn % 2 == 0, F32(1.0), F32(-1.0))

    def analyse(f, target):
        lines = 80 if column(f) else 16 * STREAMS[f][2]
        base = 1 if column(f) else 0

        def first_stage(step):
            at = pl.ds(pl.multiple_of(16 * step, 16), 16)
            for c in range(2):
                for lo in range(0, SEG, LANES):
                    hi = min(SEG, lo + LANES)
                    if column(f):
                        x = [raw_u[2 * d + c, pl.ds(2 * step, 2), :, lo:hi].reshape(16, hi - lo) for d in range(4)]
                        s02, s13 = x[0] + x[2], x[1] + x[3]
                        minus, plus = (x[3] - x[1]) * ROOT_HALF, (x[1] + x[3]) * -ROOT_HALF
                        first, final = s02 - s13, s02 + s13
                        parts = (
                            (x[0] + minus, -x[2] - plus),
                            (x[0] - x[2], x[1] - x[3]),
                            (x[0] - minus, x[2] - plus),
                        )
                    else:
                        x0, x1 = raw_x[f - 1, c, step, :, lo:hi], raw_x[f - 1, 2 + c, step, :, lo:hi]
                        final = x0 + x1
                        first, odd = final * flip, (x0 - x1) * flip
                        parts = ((odd, None), (first, None), (odd, None))
                    rows = [first]
                    for k1, (re, im) in enumerate(parts):
                        co, si = tw_ref[base, k1, 0, c, :, lo:hi], tw_ref[base, k1, 1, c, :, lo:hi]
                        if im is None:
                            rows += [re * co, -(re * si)]
                        else:
                            rows += [re * co + im * si, im * co - re * si]
                    rows.append(final)
                    for r, value in enumerate(rows):
                        high, low = split(value)
                        y_h[c, r, at, lo:hi] = high
                        y_l[c, r, at, lo:hi] = low

        each(0, lines // 16, first_stage)
        for kind, r0, r1 in ((1, 0, 7), (0, 7, 8)):
            total = None
            for c in range(2):
                high = y_h[c, r0:r1, 0:lines, :].reshape((r1 - r0) * lines, PAD)
                low = y_l[c, r0:r1, 0:lines, :].reshape((r1 - r0) * lines, PAD)
                value = dot3(
                    high, low, table[kind, c, :, 0:256], table[kind, c, :, 256:512], ((1,), (0,))
                )
                total = value if total is None else total + value
            target[r0:r1, 0:lines] = total.reshape(r1 - r0, lines, 256)

    def synthesise(f, spec):
        lines = 80 if column(f) else 16 * STREAMS[f][2]
        base = 1 if column(f) else 0
        for kind, r0, r1 in ((1, 0, 7), (0, 7, 8)):
            high, low = split(spec[r0:r1, 0:lines].reshape((r1 - r0) * lines, 256))
            both = jnp.concatenate([high, high, low], axis=1)
            for c in range(2):
                zed[c, r0:r1, 0:lines] = lax.dot_general(
                    both, table[kind, c], (((1,), (1,)), ((), ())), preferred_element_type=F32
                ).reshape(r1 - r0, lines, PAD)

        def last_stage(step):
            at = pl.ds(pl.multiple_of(8 * step, 8), 8)
            for c in range(2):
                for lo in range(0, PAD, LANES):
                    hi = lo + LANES
                    z = [zed[c, r, at, lo:hi] for r in range(8)]
                    tw = [(tw_ref[base, k1, 0, c, :, lo:hi], tw_ref[base, k1, 1, c, :, lo:hi]) for k1 in range(3)]
                    real = [z[2 * k1 + 1] * tw[k1][0] - z[2 * k1 + 2] * tw[k1][1] for k1 in range(3)]
                    if column(f):
                        (ar, br, cr) = real
                        ai, bi, ci = [z[2 * k1 + 2] * tw[k1][0] + z[2 * k1 + 1] * tw[k1][1] for k1 in range(3)]
                        up, down = z[0] + z[7], z[0] - z[7]
                        p, m = (ar - cr) * ROOT_HALF, (ai + ci) * ROOT_HALF
                        outs = (up + br + (ar + cr), -(down - bi + (p - m)), up - br + (ci - ai), (p + m) - (down + bi))
                        for d in range(4):
                            back_u[2 * d + c, step, :, lo:hi] = outs[d]
                    else:
                        even, odd = (z[0] + real[1]) * flip + z[7], (real[0] + real[2]) * flip
                        rows = pl.ds(pl.multiple_of(8 * (step % 2), 8), 8)
                        back_x[f - 1, c, step // 2, rows, lo:hi] = even + odd
                        back_x[f - 1, 2 + c, step // 2, rows, lo:hi] = even - odd

        each(0, lines // 8, last_stage)

    def send_edges(f):
        for side, sends, _ in sides(f):
            @pl.when(sends)
            def _(side=side):
                row = (64 // count(f) - 1) * (1 - side)
                at = 63 * (1 - side)
                factor = 1.0 / jnp.full((1, PAD), scale_ref[at], F32) if STREAMS[f][0] < 2 else None

                def pack(member):
                    for level in range(STREAMS[f][2]):
                        value = back(f, member)[level, row:row + 1, :]
                        edge_out(f, member)[level] = value if factor is None else value * factor

                each(0, count(f), pack)
                each(0, count(f), lambda member: edge(f, side, member).start())

    def send_back(f):
        own_scatter(f).start()
        each(1, count(f), lambda i: scatter(f, i).start())
        send_edges(f)

    def arrive(f):
        own_gather(f).wait()
        each(1, count(f), lambda i: gather(f, i).wait_recv())

    def analyse_x(f):
        arrive(f)
        analyse(f, prod_x.at[f - 1])
        for slot in (1, 0):
            for d in range(2):
                part(f, d, slot).start()

    def relay(f):
        for d in range(2):
            part(f, 1 - d, 1).wait_recv()
            at = pl.ds(pl.multiple_of(size(f) * near[d], 8), size(f))
            relay_x[f - 1, d, :, 0:size(f), :] = (
                prod_x[f - 1, 4 - 4 * d:8 - 4 * d, at, :] + part_x[f - 1, 1 - d, 1, :, 0:size(f), :]
            )
            part(f, d, 2).start()

    def add_x(f):
        for d in range(2):
            part(f, d, 0).wait_recv()
            part(f, d, 2).wait_recv()
        groups = size(f) // 8
        weights = [weights_of(16 * mine(f) + 8 * ((groups * turn + g) % 2)) for g in range(2)]
        for step in range(groups):
            at = pl.ds(pl.multiple_of(size(f) * turn + 8 * step, 8), 8)
            here = pl.ds(8 * step, 8)
            rows = []
            for r in range(8):
                d = r // 4
                value = prod_x[f - 1, r, at, :] + part_x[f - 1, d, 0, r % 4, here, :]
                rows.append(value + part_x[f - 1, 1 - d, 2, r % 4, here, :])
            for r, value in enumerate(keep(rows, weights[step % 2])):
                spec_x[f - 1, r, at, :] = value
        for d in range(2):
            whole(f, d, 0).start()

    def spread(f):
        for d in range(2):
            whole_arrival(f, d, 0).wait_recv()
        for d in range(2):
            whole(f, d, 1).start()

    def synthesise_x(f):
        for d in range(2):
            whole_arrival(f, d, 1).wait_recv()
        synthesise(f, spec_x.at[f - 1])

    analyse_x(1)
    arrive(0)
    arrive(3)
    analyse(0, prod_u)
    swap().start()
    relay(1)
    add_x(1)
    analyse_x(2)
    spread(1)
    relay(2)
    synthesise_x(1)
    send_back(1)
    add_x(2)

    swap().wait_recv()
    weights = weights_of(8 * mine(0))

    def add_u(step):
        at = pl.ds(pl.multiple_of(8 * step, 8), 8)
        rows = [prod_u[r, at, :] + peer_u[r, at, :] for r in range(8)]
        for r, value in enumerate(keep(rows, weights)):
            spec_u[r, at, :] = value

    each(0, 10, add_u)
    spread(2)
    synthesise(0, spec_u)
    send_back(0)
    send_back(3)
    synthesise_x(2)
    send_back(2)

    swap().wait_send()
    for f in (1, 0, 3, 2):
        own_scatter(f).wait()
        if not column(f):
            for d in range(2):
                for slot in range(3):
                    part(f, d, slot).wait_send()
                for slot in range(2):
                    whole(f, d, slot).wait_send()

        def finish(i, f=f):
            gather(f, i).wait_send()
            scatter(f, i).wait_send()
            scatter(f, i).wait_recv()

        each(1, count(f), finish)
        for side, sends, gets in sides(f):
            @pl.when(sends)
            def _(f=f, side=side):
                each(0, count(f), lambda member: edge(f, side, member).wait_send())

            @pl.when(gets)
            def _(f=f, side=side):
                remote(
                    edge_out(f, 0), edge_ref.at[STREAMS[f][0], side, levels(f)],
                    edge_s.at[f, 0], edge_r.at[f, side], (me + 1) % 16,
                ).wait_recv()


def stencil_kernel(
    filt_far, edge_far, tracer_far, row_scale_ref, t_far, d_far, z_far,
    filt_ref, edge_ref, tracer_ref, t_ref, d_ref, z_ref, scale_ref, inv_ref, sems, edge_sem,
):
    lat = lax.axis_index("lat")

    def arrivals(level):
        return (
            pltpu.make_async_copy(filt_far.at[:, level], filt_ref.at[:, level], sems.at[level, 0]),
            pltpu.make_async_copy(tracer_far.at[level], tracer_ref.at[level], sems.at[level, 1]),
        )

    def results(level):
        pairs = ((d_ref, d_far), (z_ref, z_far), (t_ref, t_far))
        return tuple(
            pltpu.make_async_copy(near.at[level], far.at[level], sems.at[level, 2 + k])
            for k, (near, far) in enumerate(pairs)
        )

    def fetch(level, carry):
        for copy in arrivals(level):
            copy.start()
        return carry

    edges = pltpu.make_async_copy(edge_far, edge_ref, edge_sem)
    lax.fori_loop(0, 1, fetch, 0)
    edges.start()
    lax.fori_loop(1, 8, fetch, 0)

    def spread(row, carry):
        scale_ref[pl.ds(row, 1), :] = jnp.full((1, LANES), row_scale_ref[row], F32)
        return carry

    lax.fori_loop(0, 64, spread, 0, unroll=8)
    inv_ref[...] = 1.0 / scale_ref[...]
    edges.wait()
    first = lax.broadcasted_iota(jnp.int32, (64, LANES), 0) == 0
    last = lax.broadcasted_iota(jnp.int32, (64, LANES), 0) == 63
    lane = lax.broadcasted_iota(jnp.int32, (64, LANES), 1)

    def one_level(level, carry):
        for copy in arrivals(level):
            copy.wait()
        for lo in range(0, PAD, LANES):
            hi, width = lo + LANES, min(LANES, SEG - lo)
            east, west = hi % PAD, (lo - LANES) % PAD

            def change(field, values):
                above = jnp.where(lat > 0, edge_ref[field, 0, level, :, lo:hi], F32(0.0))
                below = jnp.where(lat < 7, edge_ref[field, 1, level, :, lo:hi], F32(0.0))
                north = jnp.where(first, above, pltpu.roll(values, 1, 0))
                south = jnp.where(last, below, pltpu.roll(values, 63, 0))
                return south - north

            def east_west(field, values):
                right = jnp.where(lane == 0, filt_ref[field, level, :, east:east + LANES], values)
                left = jnp.where(lane == LANES - 1, filt_ref[field, level, :, west:west + LANES], values)
                return pltpu.roll(right, LANES - 1, 1) - pltpu.roll(left, 1, 1)

            u, v, q = (filt_ref[field, level, :, lo:hi] for field in range(3))
            scale, inv = scale_ref[...], inv_ref[...]
            d_ref[level, :, lo:lo + width] = (scale * (east_west(0, u) + change(1, v * inv)))[:, :width]
            z_ref[level, :, lo:lo + width] = (scale * (east_west(1, v) - change(0, u * inv)))[:, :width]
            flux = u * scale * east_west(2, q) + v * change(2, q)
            t_ref[level, :, lo:lo + width] = tracer_ref[level, :, lo:lo + width] - courant * flux[:, :width]
        for copy in results(level):
            copy.start()
        return carry

    def finish(level, carry):
        for copy in results(level):
            copy.wait()
        return carry

    lax.fori_loop(0, 8, one_level, 0)
    lax.fori_loop(0, 8, finish, 0)


def on_device(tables, wind_u, wind_v, tracer, cutoff, row_scale):
    coarse, fine, twiddle = (jnp.asarray(t) for t in tables)
    hbm = pl.BlockSpec(memory_space=pl.ANY)
    smem = pl.BlockSpec(memory_space=pltpu.SMEM)
    dma = pltpu.SemaphoreType.DMA
    filt, edge = pl.pallas_call(
        filter_kernel,
        name="polar_filter",
        out_shape=(
            jax.ShapeDtypeStruct((3, 8, 64, PAD), F32),
            jax.ShapeDtypeStruct((3, 2, 8, 1, PAD), F32),
        ),
        in_specs=[hbm, hbm, hbm, smem, smem, hbm, hbm, hbm],
        out_specs=(hbm, hbm),
        scratch_shapes=[
            pltpu.VMEM((8, 10, 8, SEG), F32),
            pltpu.VMEM((2, 4, 8, 16, SEG), F32),
            pltpu.VMEM((2, 2, PAD, PAD), BF16),
            pltpu.VMEM((2, 8, 128, PAD), BF16),
            pltpu.VMEM((2, 8, 128, PAD), BF16),
            pltpu.VMEM((2, 8, 128, PAD), F32),
            pltpu.VMEM((8, 80, 256), F32),
            pltpu.VMEM((8, 80, 256), F32),
            pltpu.VMEM((8, 80, 256), F32),
            pltpu.VMEM((2, 8, 128, 256), F32),
            pltpu.VMEM((2, 2, 3, 4, 32, 256), F32),
            pltpu.VMEM((2, 2, 4, 32, 256), F32),
            pltpu.VMEM((2, 8, 128, 256), F32),
            pltpu.VMEM((8, 10, 8, PAD), F32),
            pltpu.VMEM((2, 4, 8, 16, PAD), F32),
            pltpu.VMEM((8, 10, 1, PAD), F32),
            pltpu.VMEM((2, 4, 8, 1, PAD), F32),
            pltpu.VMEM((2, 2, 48, 128), F32),
            pltpu.VMEM((2, 2, 2, 32, 128), F32),
            pltpu.VMEM((2, 3, 2, 2, 1, PAD), F32),
            dma((4,)),
            dma((4, 8)), dma((4, 8)), dma, dma, dma((2, 2, 3)), dma((2, 2, 3)), dma((2, 2, 2)), dma((2, 2, 2)),
            dma((4, 8)), dma((4, 8)), dma((4, 8)), dma((4, 2)), dma((8,)),
        ],
        compiler_params=pltpu.CompilerParams(has_side_effects=True, collective_id=0, vmem_limit_bytes=60 * 1024 * 1024),
    )(wind_u, wind_v, tracer, cutoff, row_scale, coarse, fine, twiddle)
    shape = jax.ShapeDtypeStruct((8, 64, SEG), F32)
    return pl.pallas_call(
        stencil_kernel,
        name="flux_stencil",
        out_shape=(shape, shape, shape),
        in_specs=[hbm, hbm, hbm, smem],
        out_specs=(hbm, hbm, hbm),
        scratch_shapes=[
            pltpu.VMEM((3, 8, 64, PAD), F32),
            pltpu.VMEM((3, 2, 8, 1, PAD), F32),
            pltpu.VMEM((8, 64, SEG), F32),
            pltpu.VMEM((8, 64, SEG), F32),
            pltpu.VMEM((8, 64, SEG), F32),
            pltpu.VMEM((8, 64, SEG), F32),
            pltpu.VMEM((64, LANES), F32),
            pltpu.VMEM((64, LANES), F32),
            dma((8, 5)), dma,
        ],
        compiler_params=pltpu.CompilerParams(vmem_limit_bytes=60 * 1024 * 1024),
    )(filt, edge, tracer, row_scale)


def solution(mesh):
    in_specs = (
        P(None, "lat", "lon"),
        P(None, "lat", "lon"),
        P(None, "lat", "lon"),
        P("lat"),
        P("lat"),
    )
    out_specs = (P(None, "lat", "lon"), P(None, "lat", "lon"), P(None, "lat", "lon"))
    return jax.shard_map(
        functools.partial(on_device, small_tables()),
        mesh=mesh, in_specs=in_specs, out_specs=out_specs, check_vma=False,
    )
```

```python
import functools
import math

import numpy as np
import jax
import jax.numpy as jnp
from jax import lax
from jax.experimental import pallas as pl
from jax.experimental.pallas import tpu as pltpu
from jax.sharding import PartitionSpec as P

NLON = 12000
SEG = 750
PAD = 768
LANES = 128
MESH = pl.DeviceIdType.MESH
F32 = jnp.float32
BF16 = jnp.bfloat16
ROOT_HALF = math.sqrt(0.5)
courant = 0.5
STREAMS = ((0, 0, 8, True, 0), (1, 0, 8, False, 0), (2, 0, 6, False, 0), (2, 6, 2, True, 8))


def phase(steps):
    angle = 2.0 * np.pi * (np.asarray(steps, dtype=np.int64) % NLON) / NLON
    return np.stack([np.cos(angle), np.sin(angle)]).astype(np.float32)


def small_tables():
    k2 = np.arange(128)
    start = (750 * np.arange(2)[:, None] + 32 * np.arange(24)[None, :]).reshape(48)
    inner = np.arange(32)
    last = np.where(inner == 31, -1 - 736, inner)
    coarse, fine = [], []
    for mult in (8 * k2, 8 * k2 + 4):
        coarse.append(phase(start[:, None] * mult[None, :]))
        fine.append(np.stack([phase(b[:, None] * mult[None, :]) for b in (inner, last)]))
    lanes = np.arange(PAD)
    lanes = np.where(lanes == PAD - 1, -1, lanes)
    place = 750 * np.arange(2)[:, None] + lanes[None, :]
    twiddle = np.stack([np.stack([phase(k1 * (1500 * d + place)) for k1 in (1, 2, 3)]) for d in range(8)])
    return np.stack(coarse), np.stack(fine), twiddle[:, :, :, :, None, :]


def split(values):
    high = values.astype(BF16)
    return high, (values - high.astype(F32)).astype(BF16)


def dot3(high, low, table_high, table_low, dims):
    def one(a, b):
        return lax.dot_general(a, b, (dims, ((), ())), preferred_element_type=F32)

    return one(high, table_high) + (one(high, table_low) + one(low, table_high))


def filter_kernel(
    u_ref, v_ref, q_ref, cut_ref, scale_ref, coarse_far, fine_far, tw_far,
    filt_ref, edge_ref,
    raw_u, raw_x, table, y_h, y_l, zed,
    prod_u, peer_u, spec_u, prod_x, part_x, relay_x, spec_x,
    back_u, back_x, edge_u, edge_x,
    coarse_ref, fine_ref, tw_ref, seed_s,
    gather_s, gather_r, swap_s, swap_r, part_s, part_r, whole_s, whole_r,
    back_s, back_r, edge_s, edge_r, own,
):
    lat = lax.axis_index("lat")
    me = lax.axis_index("lon")
    half, turn, core = me // 8, (me // 2) % 4, me % 2
    fields = (u_ref, v_ref, q_ref)

    def column(f):
        return STREAMS[f][3]

    def count(f):
        return 8 if column(f) else 4

    def mine(f):
        return me % 8 if column(f) else 2 * half + core

    def lon_of(f, member):
        return 8 * half + member if column(f) else 8 * (member // 2) + 2 * turn + member % 2

    def levels(f):
        return pl.ds(STREAMS[f][1], STREAMS[f][2])

    def place(f):
        return pl.ds(STREAMS[f][4], STREAMS[f][2])

    def block(f, ref, member):
        rows = 64 // count(f)
        return ref.at[levels(f), pl.ds(pl.multiple_of(rows * member, rows), rows)]

    def source(f):
        return fields[STREAMS[f][0]]

    def result(f):
        return filt_ref.at[STREAMS[f][0]]

    def raw(f, member):
        return raw_u.at[member, place(f)] if column(f) else raw_x.at[f - 1, member, place(f)]

    def back(f, member):
        return back_u.at[member, place(f)] if column(f) else back_x.at[f - 1, member, place(f)]

    def edge_out(f, member):
        return edge_u.at[member, place(f)] if column(f) else edge_x.at[f - 1, member, place(f)]

    def remote(src, dst, send, recv, lon, at=None):
        place = {"lon": lon} if at is None else {"lat": at, "lon": lon}
        return pltpu.make_async_remote_copy(
            src_ref=src, dst_ref=dst, send_sem=send, recv_sem=recv, device_id=place, device_id_type=MESH
        )

    def gather(f, i):
        dest = (mine(f) + i) % count(f)
        return remote(
            block(f, source(f), dest), raw(f, mine(f)), gather_s.at[f, i], gather_r.at[f, i], lon_of(f, dest)
        )

    def own_gather(f):
        return pltpu.make_async_copy(block(f, source(f), mine(f)), raw(f, mine(f)), own.at[f])

    def scatter(f, i):
        dest = (mine(f) + i) % count(f)
        return remote(
            back(f, dest), block(f, result(f), mine(f)), back_s.at[f, i], back_r.at[f, i], lon_of(f, dest)
        )

    def own_scatter(f):
        return pltpu.make_async_copy(back(f, mine(f)), block(f, result(f), mine(f)), own.at[4 + f])

    def swap():
        return remote(prod_u, peer_u, swap_s, swap_r, (me + 8) % 16)

    odd_turn = turn % 2
    near = (turn + 1 - 2 * odd_turn, (turn + 3 + 2 * odd_turn) % 4)
    opposite = (turn + 2) % 4

    def size(f):
        return 4 * STREAMS[f][2]

    def quarter(f, ref, y, rows):
        return ref.at[f - 1, rows, pl.ds(pl.multiple_of(size(f) * y, 8), size(f))]

    def four(d):
        return pl.ds(4 * d, 4)

    def beside(d):
        return 8 * half + 2 * near[d] + core

    def part(f, d, slot):
        if slot == 2:
            src = relay_x.at[f - 1, d, :, pl.ds(0, size(f))]
        else:
            src = quarter(f, prod_x, near[d] if slot == 0 else opposite, four(d))
        return remote(
            src, part_x.at[f - 1, d, slot, :, pl.ds(0, size(f))],
            part_s.at[f - 1, d, slot], part_r.at[f - 1, d, slot], beside(d),
        )

    def whole(f, d, slot):
        if slot == 0:
            piece = quarter(f, spec_x, turn, pl.ds(0, 8))
        else:
            piece = quarter(f, spec_x, near[1 - d], four(d))
        return remote(piece, piece, whole_s.at[f - 1, d, slot], whole_r.at[f - 1, d, slot], beside(d))

    def whole_arrival(f, d, slot):
        if slot == 0:
            piece = quarter(f, spec_x, near[d], pl.ds(0, 8))
        else:
            piece = quarter(f, spec_x, opposite, four(d))
        return remote(piece, piece, whole_s.at[f - 1, d, slot], whole_r.at[f - 1, d, slot], beside(d))

    def edge(f, side, member):
        return remote(
            edge_out(f, member), edge_ref.at[STREAMS[f][0], side, levels(f)], edge_s.at[f, member], edge_r.at[f, side],
            lon_of(f, member), lat + (1 - 2 * side),
        )

    def sides(f):
        return (
            (0, jnp.logical_and(mine(f) == count(f) - 1, lat < 7), lat > 0),
            (1, jnp.logical_and(mine(f) == 0, lat > 0), lat < 7),
        )

    def each(first, last, action):
        def body(i, carry):
            action(i)
            return carry

        lax.fori_loop(first, last, body, 0)

    barrier = pltpu.get_barrier_semaphore()

    def greet(lon, at):
        pl.semaphore_signal(barrier, inc=1, device_id={"lat": at, "lon": lon}, device_id_type=MESH)

    each(1, 8, lambda i: greet(8 * half + (me + i) % 8, lat))
    for other in (core, 1 - core):
        greet(8 * (1 - half) + 2 * turn + other, lat)

    @pl.when(lat > 0)
    def _():
        greet(8 * half + 7, lat - 1)
        greet(2 * turn + 9, lat - 1)

    @pl.when(lat < 7)
    def _():
        greet(8 * half, lat + 1)
        greet(2 * turn, lat + 1)

    def either(yes):
        return jnp.where(yes, 1, 0)

    lower = 8 * either(me % 8 == 7) + 4 * either(half + core == 2)
    upper = 8 * either(me % 8 == 0) + 4 * either(half + core == 0)
    pl.semaphore_wait(barrier, 9 + lower * either(lat < 7) + upper * either(lat > 0))

    for f in (0, 3, 1, 2):
        own_gather(f).start()
        each(1, count(f), lambda i, f=f: gather(f, i).start())

    seeds = (
        pltpu.make_async_copy(coarse_far, coarse_ref, seed_s.at[0]),
        pltpu.make_async_copy(fine_far, fine_ref, seed_s.at[1]),
        pltpu.make_async_copy(tw_far.at[turn], tw_ref.at[0], seed_s.at[2]),
        pltpu.make_async_copy(tw_far.at[4 * half], tw_ref.at[1], seed_s.at[3]),
    )
    for seed in seeds:
        seed.start()
    for seed in seeds:
        seed.wait()

    for kind in range(2):
        for c in range(2):
            def fill(a, kind=kind, c=c):
                tail = jnp.where(a == 23, 1, 0)
                c1 = coarse_ref[kind, 0, pl.ds(24 * c + a, 1), :]
                s1 = coarse_ref[kind, 1, pl.ds(24 * c + a, 1), :]
                c2 = fine_ref[kind, tail, 0]
                s2 = fine_ref[kind, tail, 1]
                rows = pl.ds(pl.multiple_of(32 * a, 32), 32)
                for side, value in enumerate((c1 * c2 - s1 * s2, s1 * c2 + c1 * s2)):
                    high, low = split(value)
                    table[kind, c, rows, pl.ds(128 * side, 128)] = high
                    table[kind, c, rows, pl.ds(256 + 128 * side, 128)] = low
                    table[kind, c, rows, pl.ds(512 + 128 * side, 128)] = high

            each(0, 24, fill)
    for r in range(8):
        for c in range(2):
            y_h[c, r, :, 640:] = jnp.zeros((128, 128), BF16)
            y_l[c, r, :, 640:] = jnp.zeros((128, 128), BF16)

    row_at = lax.broadcasted_iota(jnp.int32, (8, 256), 0)
    lane_at = lax.broadcasted_iota(jnp.int32, (8, 256), 1)
    k2 = lane_at % 128
    sign = jnp.where(lane_at < 128, 1.0, -1.0).astype(F32)
    zero = jnp.where(k2 == 0, F32(0.5), F32(1.0))

    def limits_of(first):
        limits = jnp.zeros((8, 256), jnp.int32)
        for row in range(8):
            limits = jnp.where(row_at == row, cut_ref[first + row], limits)
        return limits

    def weights_of(first):
        limits = limits_of(first)

        def kept(k):
            return jnp.where(k < limits, F32(2.0 / NLON), F32(0.0))

        pairs = []
        for k1 in (1, 2, 3):
            above, below = kept(8 * k2 + 4 + k1), kept(8 * k2 + 4 - k1)
            pairs.append((above + below, (above - below) * sign))
        return kept(8 * k2 + 4), kept(8 * k2) * zero, pairs

    def keep(rows, weights):
        centre, single, pairs = weights
        out = [rows[0] * centre]
        for k1 in (1, 2, 3):
            both, odd = pairs[k1 - 1]
            r1, r2 = rows[2 * k1 - 1], rows[2 * k1]
            swap1 = jnp.concatenate([r1[:, 128:], r1[:, :128]], axis=1)
            swap2 = jnp.concatenate([r2[:, 128:], r2[:, :128]], axis=1)
            out += [both * r1 + odd * swap2, both * r2 - odd * swap1]
        return out + [rows[7] * single]

    flip = jnp.where(turn % 2 == 0, F32(1.0), F32(-1.0))

    def analyse(f, target):
        lines = 80 if column(f) else 16 * STREAMS[f][2]
        base = 1 if column(f) else 0

        def first_stage(step):
            at = pl.ds(pl.multiple_of(16 * step, 16), 16)
            for c in range(2):
                for lo in range(0, SEG, LANES):
                    hi = min(SEG, lo + LANES)
                    if column(f):
                        x = [raw_u[2 * d + c, pl.ds(2 * step, 2), :, lo:hi].reshape(16, hi - lo) for d in range(4)]
                        s02, s13 = x[0] + x[2], x[1] + x[3]
                        minus, plus = (x[3] - x[1]) * ROOT_HALF, (x[1] + x[3]) * -ROOT_HALF
                        first, final = s02 - s13, s02 + s13
                        parts = (
                            (x[0] + minus, -x[2] - plus),
                            (x[0] - x[2], x[1] - x[3]),
                            (x[0] - minus, x[2] - plus),
                        )
                    else:
                        x0, x1 = raw_x[f - 1, c, step, :, lo:hi], raw_x[f - 1, 2 + c, step, :, lo:hi]
                        final = x0 + x1
                        first, odd = final * flip, (x0 - x1) * flip
                        parts = ((odd, None), (first, None), (odd, None))
                    rows = [first]
                    for k1, (re, im) in enumerate(parts):
                        co, si = tw_ref[base, k1, 0, c, :, lo:hi], tw_ref[base, k1, 1, c, :, lo:hi]
                        if im is None:
                            rows += [re * co, -(re * si)]
                        else:
                            rows += [re * co + im * si, im * co - re * si]
                    rows.append(final)
                    for r, value in enumerate(rows):
                        high, low = split(value)
                        y_h[c, r, at, lo:hi] = high
                        y_l[c, r, at, lo:hi] = low

        each(0, lines // 16, first_stage)
        for kind, r0, r1 in ((1, 0, 7), (0, 7, 8)):
            total = None
            for c in range(2):
                high = y_h[c, r0:r1, 0:lines, :].reshape((r1 - r0) * lines, PAD)
                low = y_l[c, r0:r1, 0:lines, :].reshape((r1 - r0) * lines, PAD)
                value = dot3(
                    high, low, table[kind, c, :, 0:256], table[kind, c, :, 256:512], ((1,), (0,))
                )
                total = value if total is None else total + value
            target[r0:r1, 0:lines] = total.reshape(r1 - r0, lines, 256)

    def synthesise(f, spec):
        lines = 80 if column(f) else 16 * STREAMS[f][2]
        base = 1 if column(f) else 0
        for kind, r0, r1 in ((1, 0, 7), (0, 7, 8)):
            high, low = split(spec[r0:r1, 0:lines].reshape((r1 - r0) * lines, 256))
            both = jnp.concatenate([high, high, low], axis=1)
            for c in range(2):
                zed[c, r0:r1, 0:lines] = lax.dot_general(
                    both, table[kind, c], (((1,), (1,)), ((), ())), preferred_element_type=F32
                ).reshape(r1 - r0, lines, PAD)

        def last_stage(step):
            at = pl.ds(pl.multiple_of(8 * step, 8), 8)
            for c in range(2):
                for lo in range(0, PAD, LANES):
                    hi = lo + LANES
                    z = [zed[c, r, at, lo:hi] for r in range(8)]
                    tw = [(tw_ref[base, k1, 0, c, :, lo:hi], tw_ref[base, k1, 1, c, :, lo:hi]) for k1 in range(3)]
                    real = [z[2 * k1 + 1] * tw[k1][0] - z[2 * k1 + 2] * tw[k1][1] for k1 in range(3)]
                    if column(f):
                        (ar, br, cr) = real
                        ai, bi, ci = [z[2 * k1 + 2] * tw[k1][0] + z[2 * k1 + 1] * tw[k1][1] for k1 in range(3)]
                        up, down = z[0] + z[7], z[0] - z[7]
                        p, m = (ar - cr) * ROOT_HALF, (ai + ci) * ROOT_HALF
                        outs = (up + br + (ar + cr), -(down - bi + (p - m)), up - br + (ci - ai), (p + m) - (down + bi))
                        for d in range(4):
                            back_u[2 * d + c, step, :, lo:hi] = outs[d]
                    else:
                        even, odd = (z[0] + real[1]) * flip + z[7], (real[0] + real[2]) * flip
                        rows = pl.ds(pl.multiple_of(8 * (step % 2), 8), 8)
                        back_x[f - 1, c, step // 2, rows, lo:hi] = even + odd
                        back_x[f - 1, 2 + c, step // 2, rows, lo:hi] = even - odd

        each(0, lines // 8, last_stage)

    def send_edges(f):
        for side, sends, _ in sides(f):
            @pl.when(sends)
            def _(side=side):
                row = (64 // count(f) - 1) * (1 - side)
                at = 63 * (1 - side)
                factor = 1.0 / jnp.full((1, PAD), scale_ref[at], F32) if STREAMS[f][0] < 2 else None

                def pack(member):
                    for level in range(STREAMS[f][2]):
                        value = back(f, member)[level, row:row + 1, :]
                        edge_out(f, member)[level] = value if factor is None else value * factor

                each(0, count(f), pack)
                each(0, count(f), lambda member: edge(f, side, member).start())

    def send_back(f):
        own_scatter(f).start()
        each(1, count(f), lambda i: scatter(f, i).start())
        send_edges(f)

    def arrive(f):
        own_gather(f).wait()
        each(1, count(f), lambda i: gather(f, i).wait_recv())

    def analyse_x(f):
        arrive(f)
        analyse(f, prod_x.at[f - 1])
        for slot in (1, 0):
            for d in range(2):
                part(f, d, slot).start()

    def relay(f):
        for d in range(2):
            part(f, 1 - d, 1).wait_recv()
            at = pl.ds(pl.multiple_of(size(f) * near[d], 8), size(f))
            relay_x[f - 1, d, :, 0:size(f), :] = (
                prod_x[f - 1, 4 - 4 * d:8 - 4 * d, at, :] + part_x[f - 1, 1 - d, 1, :, 0:size(f), :]
            )
            part(f, d, 2).start()

    def add_x(f):
        for d in range(2):
            part(f, d, 0).wait_recv()
            part(f, d, 2).wait_recv()
        groups = size(f) // 8
        weights = [weights_of(16 * mine(f) + 8 * ((groups * turn + g) % 2)) for g in range(2)]
        for step in range(groups):
            at = pl.ds(pl.multiple_of(size(f) * turn + 8 * step, 8), 8)
            here = pl.ds(8 * step, 8)
            rows = []
            for r in range(8):
                d = r // 4
                value = prod_x[f - 1, r, at, :] + part_x[f - 1, d, 0, r % 4, here, :]
                rows.append(value + part_x[f - 1, 1 - d, 2, r % 4, here, :])
            for r, value in enumerate(keep(rows, weights[step % 2])):
                spec_x[f - 1, r, at, :] = value
        for d in range(2):
            whole(f, d, 0).start()

    def spread(f):
        for d in range(2):
            whole_arrival(f, d, 0).wait_recv()
        for d in range(2):
            whole(f, d, 1).start()

    def synthesise_x(f):
        for d in range(2):
            whole_arrival(f, d, 1).wait_recv()
        synthesise(f, spec_x.at[f - 1])

    analyse_x(1)
    arrive(0)
    arrive(3)
    analyse(0, prod_u)
    swap().start()
    relay(1)
    add_x(1)
    analyse_x(2)
    spread(1)
    relay(2)
    synthesise_x(1)
    send_back(1)
    add_x(2)

    swap().wait_recv()
    weights = weights_of(8 * mine(0))

    def add_u(step):
        at = pl.ds(pl.multiple_of(8 * step, 8), 8)
        rows = [prod_u[r, at, :] + peer_u[r, at, :] for r in range(8)]
        for r, value in enumerate(keep(rows, weights)):
            spec_u[r, at, :] = value

    each(0, 10, add_u)
    spread(2)
    synthesise(0, spec_u)
    send_back(0)
    send_back(3)
    synthesise_x(2)
    send_back(2)

    swap().wait_send()
    for f in (0, 3, 1, 2):
        own_scatter(f).wait()
        if not column(f):
            for d in range(2):
                for slot in range(3):
                    part(f, d, slot).wait_send()
                for slot in range(2):
                    whole(f, d, slot).wait_send()

        def finish(i, f=f):
            gather(f, i).wait_send()
            scatter(f, i).wait_send()
            scatter(f, i).wait_recv()

        each(1, count(f), finish)
        for side, sends, gets in sides(f):
            @pl.when(sends)
            def _(f=f, side=side):
                each(0, count(f), lambda member: edge(f, side, member).wait_send())

            @pl.when(gets)
            def _(f=f, side=side):
                remote(
                    edge_out(f, 0), edge_ref.at[STREAMS[f][0], side, levels(f)],
                    edge_s.at[f, 0], edge_r.at[f, side], (me + 1) % 16,
                ).wait_recv()


def stencil_kernel(
    filt_far, edge_far, tracer_far, row_scale_ref, t_far, d_far, z_far,
    filt_ref, edge_ref, tracer_ref, t_ref, d_ref, z_ref, scale_ref, inv_ref, sems, edge_sem,
):
    lat = lax.axis_index("lat")

    def arrivals(level):
        return (
            pltpu.make_async_copy(filt_far.at[:, level], filt_ref.at[:, level], sems.at[level, 0]),
            pltpu.make_async_copy(tracer_far.at[level], tracer_ref.at[level], sems.at[level, 1]),
        )

    def results(level):
        pairs = ((d_ref, d_far), (z_ref, z_far), (t_ref, t_far))
        return tuple(
            pltpu.make_async_copy(near.at[level], far.at[level], sems.at[level, 2 + k])
            for k, (near, far) in enumerate(pairs)
        )

    def fetch(level, carry):
        for copy in arrivals(level):
            copy.start()
        return carry

    edges = pltpu.make_async_copy(edge_far, edge_ref, edge_sem)
    lax.fori_loop(0, 1, fetch, 0)
    edges.start()
    lax.fori_loop(1, 8, fetch, 0)

    def spread(row, carry):
        scale_ref[pl.ds(row, 1), :] = jnp.full((1, LANES), row_scale_ref[row], F32)
        return carry

    lax.fori_loop(0, 64, spread, 0, unroll=8)
    inv_ref[...] = 1.0 / scale_ref[...]
    edges.wait()
    first = lax.broadcasted_iota(jnp.int32, (64, LANES), 0) == 0
    last = lax.broadcasted_iota(jnp.int32, (64, LANES), 0) == 63
    lane = lax.broadcasted_iota(jnp.int32, (64, LANES), 1)

    def one_level(level, carry):
        for copy in arrivals(level):
            copy.wait()
        for lo in range(0, PAD, LANES):
            hi, width = lo + LANES, min(LANES, SEG - lo)
            east, west = hi % PAD, (lo - LANES) % PAD

            def change(field, values):
                above = jnp.where(lat > 0, edge_ref[field, 0, level, :, lo:hi], F32(0.0))
                below = jnp.where(lat < 7, edge_ref[field, 1, level, :, lo:hi], F32(0.0))
                north = jnp.where(first, above, pltpu.roll(values, 1, 0))
                south = jnp.where(last, below, pltpu.roll(values, 63, 0))
                return south - north

            def east_west(field, values):
                right = jnp.where(lane == 0, filt_ref[field, level, :, east:east + LANES], values)
                left = jnp.where(lane == LANES - 1, filt_ref[field, level, :, west:west + LANES], values)
                return pltpu.roll(right, LANES - 1, 1) - pltpu.roll(left, 1, 1)

            u, v, q = (filt_ref[field, level, :, lo:hi] for field in range(3))
            scale, inv = scale_ref[...], inv_ref[...]
            d_ref[level, :, lo:lo + width] = (scale * (east_west(0, u) + change(1, v * inv)))[:, :width]
            z_ref[level, :, lo:lo + width] = (scale * (east_west(1, v) - change(0, u * inv)))[:, :width]
            flux = u * scale * east_west(2, q) + v * change(2, q)
            t_ref[level, :, lo:lo + width] = tracer_ref[level, :, lo:lo + width] - courant * flux[:, :width]
        for copy in results(level):
            copy.start()
        return carry

    def finish(level, carry):
        for copy in results(level):
            copy.wait()
        return carry

    lax.fori_loop(0, 8, one_level, 0)
    lax.fori_loop(0, 8, finish, 0)


def on_device(tables, wind_u, wind_v, tracer, cutoff, row_scale):
    coarse, fine, twiddle = (jnp.asarray(t) for t in tables)
    hbm = pl.BlockSpec(memory_space=pl.ANY)
    smem = pl.BlockSpec(memory_space=pltpu.SMEM)
    dma = pltpu.SemaphoreType.DMA
    filt, edge = pl.pallas_call(
        filter_kernel,
        name="polar_filter",
        out_shape=(
            jax.ShapeDtypeStruct((3, 8, 64, PAD), F32),
            jax.ShapeDtypeStruct((3, 2, 8, 1, PAD), F32),
        ),
        in_specs=[hbm, hbm, hbm, smem, smem, hbm, hbm, hbm],
        out_specs=(hbm, hbm),
        scratch_shapes=[
            pltpu.VMEM((8, 10, 8, SEG), F32),
            pltpu.VMEM((2, 4, 8, 16, SEG), F32),
            pltpu.VMEM((2, 2, PAD, PAD), BF16),
            pltpu.VMEM((2, 8, 128, PAD), BF16),
            pltpu.VMEM((2, 8, 128, PAD), BF16),
            pltpu.VMEM((2, 8, 128, PAD), F32),
            pltpu.VMEM((8, 80, 256), F32),
            pltpu.VMEM((8, 80, 256), F32),
            pltpu.VMEM((8, 80, 256), F32),
            pltpu.VMEM((2, 8, 128, 256), F32),
            pltpu.VMEM((2, 2, 3, 4, 32, 256), F32),
            pltpu.VMEM((2, 2, 4, 32, 256), F32),
            pltpu.VMEM((2, 8, 128, 256), F32),
            pltpu.VMEM((8, 10, 8, PAD), F32),
            pltpu.VMEM((2, 4, 8, 16, PAD), F32),
            pltpu.VMEM((8, 10, 1, PAD), F32),
            pltpu.VMEM((2, 4, 8, 1, PAD), F32),
            pltpu.VMEM((2, 2, 48, 128), F32),
            pltpu.VMEM((2, 2, 2, 32, 128), F32),
            pltpu.VMEM((2, 3, 2, 2, 1, PAD), F32),
            dma((4,)),
            dma((4, 8)), dma((4, 8)), dma, dma, dma((2, 2, 3)), dma((2, 2, 3)), dma((2, 2, 2)), dma((2, 2, 2)),
            dma((4, 8)), dma((4, 8)), dma((4, 8)), dma((4, 2)), dma((8,)),
        ],
        compiler_params=pltpu.CompilerParams(has_side_effects=True, collective_id=0, vmem_limit_bytes=60 * 1024 * 1024),
    )(wind_u, wind_v, tracer, cutoff, row_scale, coarse, fine, twiddle)
    shape = jax.ShapeDtypeStruct((8, 64, SEG), F32)
    return pl.pallas_call(
        stencil_kernel,
        name="flux_stencil",
        out_shape=(shape, shape, shape),
        in_specs=[hbm, hbm, hbm, smem],
        out_specs=(hbm, hbm, hbm),
        scratch_shapes=[
            pltpu.VMEM((3, 8, 64, PAD), F32),
            pltpu.VMEM((3, 2, 8, 1, PAD), F32),
            pltpu.VMEM((8, 64, SEG), F32),
            pltpu.VMEM((8, 64, SEG), F32),
            pltpu.VMEM((8, 64, SEG), F32),
            pltpu.VMEM((8, 64, SEG), F32),
            pltpu.VMEM((64, LANES), F32),
            pltpu.VMEM((64, LANES), F32),
            dma((8, 5)), dma,
        ],
        compiler_params=pltpu.CompilerParams(vmem_limit_bytes=60 * 1024 * 1024),
    )(filt, edge, tracer, row_scale)


def solution(mesh):
    in_specs = (
        P(None, "lat", "lon"),
        P(None, "lat", "lon"),
        P(None, "lat", "lon"),
        P("lat"),
        P("lat"),
    )
    out_specs = (P(None, "lat", "lon"), P(None, "lat", "lon"), P(None, "lat", "lon"))
    return jax.shard_map(
        functools.partial(on_device, small_tables()),
        mesh=mesh, in_specs=in_specs, out_specs=out_specs, check_vma=False,
    )
```
